32 devices in a mesh: space: 16 (over z, y, x), phase: 2 (over core).
Axes of the slice: x: 2, y: 2, z: 4, core: 2. Of those that a mesh axis runs over, the one named last changes fastest.
Arguments:
- particle_cell: int32 [2, 1024, 128], P('phase', 'space'), may hold values from 0 to 63
- block_count: int32 [2, 1024], P('phase', 'space'), may hold values from 1 to 128, as said below
- particle_frac: float32 [2, 3, 1024, 128], P('phase', None, 'space'), may hold values from 0 to 1
- particle_vel: float32 [2, 3, 1024, 128], P('phase', None, 'space'), may hold values from -2.5 to 2.5
- particle_mass: float32 [2, 1024, 128], P('phase', 'space'), may hold values from 0.5 to 2
- particle_stress: float32 [2, 1024, 128], P('phase', 'space'), may hold values from -6 to 6
- drag_coef: float32 [64, 8, 128], P('space'), may hold values from 0.2 to 5
Outputs:
- frac_out: float32 [2, 3, 1024, 128], P('phase', None, 'space')
- vel_out: float32 [2, 3, 1024, 128], P('phase', None, 'space')
- stress_out: float32 [2, 1024, 128], P('phase', 'space')
The draws below stay inside these ranges and needn't reach their ends.
Inputs may be any that keep to these rules, and one draw needn't show every extreme that they name: `particle_cell`: the cell of a slot within its block of 4 x 4 x 4 cells, numbered 16 a + 4 b + c for the offsets a, b, c along the first, second and third dimension. `block_count`: slots 0 to count - 1 of a block hold particles, the others are empty; among the blocks b with the same b // 64 in a phase, one has all 128 slots live.
All inputs are finite; a program needn't handle non-finite values.
Results may differ from the reference program's by a relative error of at most 0.0003.
Values sent between devices are 32-bit elements; how exact they have to be, the bound alone decides.
No kernel may reach another device: no remote copies, remote signals or barrier semaphores. Data moves between devices by JAX's collectives and lax.ppermute only.
A program may use at most 64 MiB of HBM per device.

```python
import math
import jax
import jax.numpy as jnp
from jax import lax

NBY = 2
NBZ = 32
SLOTS = 128
OUTER = 1
SUBSTEPS = 2
NB = 64
BLOCKS = 1024
PHASES = 2
NX = 64
NY = 8
NZ = 128
N_SPACE = 16


def draw_block_count(key, part):
    base_key = jax.random.fold_in(key, 7177)
    level_key, count_key, full_key = jax.random.split(base_key, 3)
    ndevice = BLOCKS // NB
    level_shift = jax.random.randint(level_key, (PHASES, ndevice, 1), 0, 4)
    load_level = jnp.right_shift(jnp.full((PHASES, ndevice, 1), SLOTS, jnp.int32), level_shift)
    lowest = load_level // 2
    raw_draw = jax.random.randint(count_key, (PHASES, ndevice, NB), 0, 1 << 30)
    counts = lowest + raw_draw % (load_level - lowest + 1)
    full_block = jax.random.randint(full_key, (PHASES, ndevice, 1), 0, NB)
    block_ids = jnp.arange(NB, dtype=jnp.int32)[None, None, :]
    counts = jnp.where(block_ids == full_block, SLOTS, counts)
    return counts.reshape(PHASES, BLOCKS).astype(jnp.int32)


def place_ends(drawn, rng, smallest, top_value):
    longest = drawn.shape.index(max(drawn.shape))
    spots = []
    for shift in (0, 1):
        where = [jax.random.randint(jax.random.fold_in(rng, axis), (), 0, length) for axis, length in enumerate(drawn.shape)]
        where[longest] = (where[longest] + shift) % drawn.shape[longest]
        spots.append(tuple(where))
    return drawn.at[spots[0]].set(smallest).at[spots[1]].set(top_value)


def steps_of(rng, dims, shards, low, largest):
    factor_of, own = 1.0, jax.random.fold_in(rng, 6)
    for dim, parts in shards:
        steps = jnp.exp(jax.random.uniform(jax.random.fold_in(own, dim), (parts,), jnp.float32, low / len(shards), largest / len(shards)))
        factor_of = factor_of * jnp.repeat(steps, dims[dim] // parts).reshape([-1 if axis == dim else 1 for axis in range(len(dims))])
    return factor_of


def noise(rng, dims, deviation, bound, cuts=(), kind=jnp.bfloat16):
    level = steps_of(rng, dims, cuts, -0.22, 0.18) if cuts else 1.0
    values = jax.random.normal(rng, dims, jnp.float32) * deviation * level
    return jnp.minimum(jnp.maximum(values, -bound), bound).astype(kind)


def setup_inputs(seed: int = 0) -> dict:
    seeds = jax.random.split(jax.random.key(seed), 8)
    particle_cell = place_ends(jax.random.randint(seeds[0], (PHASES, BLOCKS, SLOTS), 0, 64), jax.random.fold_in(seeds[0], 1), 0, 63).astype(jnp.int32)
    block_count = draw_block_count(jax.random.fold_in(seeds[7], 71), 0)
    particle_frac = jnp.clip(1.0 * jax.random.uniform(seeds[2], (PHASES, 3, BLOCKS, SLOTS), jnp.float32) ** steps_of(seeds[2], (PHASES, 3, BLOCKS, SLOTS), ((0, 2), (2, 16)), -0.2, 0.2), 0.0, 1.0)
    particle_vel = noise(seeds[3], (PHASES, 3, BLOCKS, SLOTS), 0.5, 2.5, ((0, 2), (2, 16)), jnp.float32)
    particle_mass = jnp.clip(jnp.exp(math.log(2.0) - 1.3862944 * jax.random.uniform(seeds[4], (PHASES, BLOCKS, SLOTS), jnp.float32) ** steps_of(seeds[4], (PHASES, BLOCKS, SLOTS), ((0, 2), (1, 16)), -0.2, 0.2)), 0.5, 2.0)
    particle_stress = noise(seeds[5], (PHASES, BLOCKS, SLOTS), 1.0, 6.0, ((0, 2), (1, 16)), jnp.float32)
    drag_coef = jnp.clip(jnp.exp(math.log(5.0) - 3.218876 * jax.random.uniform(seeds[6], (NX, NY, NZ), jnp.float32) ** steps_of(seeds[6], (NX, NY, NZ), ((0, 16),), -0.2, 0.2)), 0.2, 5.0)
    return {"particle_cell": particle_cell, "block_count": block_count, "particle_frac": particle_frac, "particle_vel": particle_vel, "particle_mass": particle_mass, "particle_stress": particle_stress, "drag_coef": drag_coef}


time_step = 0.05
gravity = 1.0
bulk_modulus = 4.0
mass_floor = 0.25
slip_floor = 0.25
highest = lax.Precision.HIGHEST

def intersection_add(array, axis):
    moved_arr = jnp.moveaxis(array, (axis, axis + 1), (-2, -1))
    nblock = moved_arr.shape[-2]
    leading = moved_arr.shape[:-2]
    flat_pad = [(0, 0)] * len(leading)
    main_part = moved_arr[..., :4].reshape(leading + (4 * nblock,))
    main_part = jnp.pad(main_part, flat_pad + [(0, 2)])
    tail_part = jnp.pad(moved_arr[..., 4:], flat_pad + [(0, 0), (0, 2)])
    tail_part = tail_part.reshape(leading + (4 * nblock,))
    tail_part = jnp.pad(tail_part, flat_pad + [(4, 0)])[..., :4 * nblock + 2]
    return jnp.moveaxis(main_part + tail_part, -1, axis)

def cut_windows(array, axis):
    moved_arr = jnp.moveaxis(array, axis, -1)
    nblock = (moved_arr.shape[-1] - 2) // 4
    leading = moved_arr.shape[:-1]
    main_part = moved_arr[..., :4 * nblock].reshape(leading + (nblock, 4))
    tail_part = jnp.pad(moved_arr[..., 4:], [(0, 0)] * len(leading) + [(0, 2)])
    tail_part = tail_part.reshape(leading + (nblock, 4))[..., :2]
    tile_set = jnp.concatenate([main_part, tail_part], axis=-1)
    return jnp.moveaxis(tile_set, (-2, -1), (axis, axis + 1))

def axis_factors(offset, within):
    relative = within - 0.5
    weights = (0.5 * (0.5 - relative) * (0.5 - relative), 0.75 - relative * relative, 0.5 * (0.5 + relative) * (0.5 + relative))
    places = lax.broadcasted_iota(jnp.int32, (1, 6, 1), 1)
    result = jnp.zeros(offset.shape[:1] + (6,) + offset.shape[1:], within.dtype)
    for stencil, weight in enumerate(weights):
        result = result + jnp.where(places == offset[:, None, :] + stencil, weight[:, None, :], 0.0)
    return result

def particle_frame(cell_ids, frac_part, counts):
    nblocks, slot_count = cell_ids.shape
    is_live = lax.broadcasted_iota(jnp.int32, (nblocks, slot_count), 1) < counts[:, None]
    offset_x = cell_ids // 16
    offset_y = cell_ids // 4 % 4
    offset_z = cell_ids % 4
    block_ids = lax.broadcasted_iota(jnp.int32, (nblocks, slot_count), 0)
    start_y = 4 * (block_ids // NBZ)
    start_z = 4 * (block_ids % NBZ)
    position = jnp.stack([offset_x + frac_part[0], start_y + offset_y + frac_part[1], start_z + offset_z + frac_part[2]])
    return (is_live, (offset_x, offset_y, offset_z), position)

def node_coords(rows_y, rows_z, float_type):
    return (jnp.arange(6, dtype=float_type).reshape(6, 1, 1) - 0.5, jnp.arange(rows_y, dtype=float_type).reshape(1, rows_y, 1) + 0.5, jnp.arange(rows_z, dtype=float_type).reshape(1, 1, rows_z) + 0.5)

def plane_factors(offsets, frac_part):
    factor_x = axis_factors(offsets[0], frac_part[0])
    factor_y = axis_factors(offsets[1], frac_part[1])
    factor_z = axis_factors(offsets[2], frac_part[2])
    plane_xy = (factor_x[:, :, None] * factor_y[:, None]).reshape(factor_x.shape[0], 36, -1)
    return (plane_xy, factor_z)

def deposit(cell_ids, frac_part, velocity, node_mass_in, pressure, counts):
    is_live, offsets, position = particle_frame(cell_ids, frac_part, counts)
    mass_live = jnp.where(is_live, node_mass_in, 0.0)
    loaded = jnp.where(is_live, pressure, 0.0)
    channels = jnp.stack([mass_live, mass_live * velocity[0], mass_live * velocity[1], mass_live * velocity[2], loaded, loaded * position[0], loaded * position[1], loaded * position[2]], axis=1)
    plane_xy, factor_z = plane_factors(offsets, frac_part)
    column = (channels[:, :, None] * factor_z[:, None]).reshape(channels.shape[0], 48, -1)
    tile_set = jnp.einsum('gap,gmp->gam', plane_xy, column, precision=highest)
    tile_set = tile_set.reshape(NBY, NBZ, 6, 6, 8, 6).transpose(4, 2, 0, 3, 1, 5)
    summed = intersection_add(intersection_add(tile_set, 4), 2)[:, :, 1:-1, 1:-1]
    node_pos = node_coords(summed.shape[2], summed.shape[3], summed.dtype)
    momentum = [summed[1 + axis_id] + 4.0 * time_step * (node_pos[axis_id] * summed[4] - summed[5 + axis_id]) for axis_id in range(3)]
    return jnp.stack([summed[0]] + momentum)

def grid_velocity(fields):
    velocity = fields[1:4] / jnp.maximum(fields[0], mass_floor)
    lifted = velocity[2] - time_step * gravity
    floor_mask = lax.broadcasted_iota(jnp.int32, lifted.shape, 2) == 0
    lifted = jnp.where(floor_mask, jnp.maximum(lifted, 0.0), lifted)
    return jnp.stack([velocity[0], velocity[1], lifted])

def apply_drag(velocity, node_mass, other_velocity, other_mass, coefficient):
    slip_vel = other_velocity - velocity
    slip_speed = jnp.sqrt(lax.optimization_barrier(jnp.sum(slip_vel * slip_vel, axis=0)) + slip_floor)
    drag_rate = coefficient * slip_speed
    mass_share = other_mass / (node_mass + other_mass + mass_floor)
    return velocity + drag_rate / (1.0 + drag_rate) * mass_share * slip_vel

def gather_back(grid_vel, cell_ids, frac_part, velocity, pressure, counts):
    is_live, offsets, position = particle_frame(cell_ids, frac_part, counts)
    node_pos = node_coords(grid_vel.shape[2], grid_vel.shape[3], grid_vel.dtype)
    dotted = node_pos[0] * grid_vel[0] + node_pos[1] * grid_vel[1] + node_pos[2] * grid_vel[2]
    fields = jnp.concatenate([grid_vel, dotted[None]], axis=0)
    fields = jnp.pad(fields, ((0, 0), (0, 0), (1, 1), (1, 1)))
    tile_set = cut_windows(cut_windows(fields, 3), 2)
    tile_set = tile_set.transpose(2, 4, 1, 3, 0, 5).reshape(NBY * NBZ, 36, 24)
    plane_xy, factor_z = plane_factors(offsets, frac_part)
    spread = jnp.einsum('gam,gap->gmp', tile_set, plane_xy, precision=highest)
    spread = spread.reshape(tile_set.shape[0], 4, 6, -1)
    sampled = lax.optimization_barrier(jnp.sum(spread * factor_z[:, None], axis=2))
    sampled = jnp.moveaxis(sampled, 1, 0)
    new_vel = sampled[:3]
    spread_rate = 4.0 * (sampled[3] - lax.optimization_barrier(jnp.sum(position * new_vel, axis=0)))
    out_frac = jnp.where(is_live[None], frac_part + time_step * new_vel, frac_part)
    out_vel = jnp.where(is_live[None], new_vel, velocity)
    out_stress = jnp.where(is_live, pressure - time_step * bulk_modulus * spread_rate, pressure)
    return (out_frac, out_vel, out_stress)

def reference(particle_cell, block_count, particle_frac, particle_vel, particle_mass, particle_stress, drag_coef):
    nblock = NBY * NBZ
    cell_parts = [particle_cell[phase_id].reshape(N_SPACE, nblock, SLOTS) for phase_id in range(2)]
    count_parts = [block_count[phase_id].reshape(N_SPACE, nblock) for phase_id in range(2)]
    frac_parts = [jnp.moveaxis(particle_frac[phase_id].reshape(3, N_SPACE, nblock, SLOTS), 1, 0) for phase_id in range(2)]
    vel_parts = [jnp.moveaxis(particle_vel[phase_id].reshape(3, N_SPACE, nblock, SLOTS), 1, 0) for phase_id in range(2)]
    mass_parts = [particle_mass[phase_id].reshape(N_SPACE, nblock, SLOTS) for phase_id in range(2)]
    stress_parts = [particle_stress[phase_id].reshape(N_SPACE, nblock, SLOTS) for phase_id in range(2)]
    for outer_step in range(OUTER):
        for sub_step in range(SUBSTEPS):
            grid_list = []
            for phase_id in range(2):
                deposits = lax.map(lambda packed: deposit(packed[0], packed[1], packed[2], packed[3], packed[4], packed[5]), (cell_parts[phase_id], frac_parts[phase_id], vel_parts[phase_id], mass_parts[phase_id], stress_parts[phase_id], count_parts[phase_id]))
                fields = intersection_add(jnp.moveaxis(deposits, 0, 1), 1)[:, 1:-1]
                grid_list.append((fields[0], grid_velocity(fields)))
            if sub_step == 0:
                solid_vel = apply_drag(grid_list[0][1], grid_list[0][0], grid_list[1][1], grid_list[1][0], drag_coef)
                water_vel = apply_drag(grid_list[1][1], grid_list[1][0], grid_list[0][1], grid_list[0][0], drag_coef)
                velocities = [solid_vel, water_vel]
            else:
                velocities = [grid_list[0][1], grid_list[1][1]]
            for phase_id in range(2):
                padded = jnp.pad(velocities[phase_id], ((0, 0), (1, 1), (0, 0), (0, 0)))
                windows = jnp.moveaxis(cut_windows(padded, 1), 1, 0)
                new_state = lax.map(lambda packed: gather_back(packed[0], packed[1], packed[2], packed[3], packed[4], packed[5]), (windows, cell_parts[phase_id], frac_parts[phase_id], vel_parts[phase_id], stress_parts[phase_id], count_parts[phase_id]))
                frac_parts[phase_id] = new_state[0]
                vel_parts[phase_id] = new_state[1]
                stress_parts[phase_id] = new_state[2]
    frac_out = jnp.stack([jnp.moveaxis(frac_parts[phase_id], 0, 1).reshape(3, N_SPACE * nblock, SLOTS) for phase_id in range(2)])
    vel_out = jnp.stack([jnp.moveaxis(vel_parts[phase_id], 0, 1).reshape(3, N_SPACE * nblock, SLOTS) for phase_id in range(2)])
    stress_out = jnp.stack([stress_parts[phase_id].reshape(N_SPACE * nblock, SLOTS) for phase_id in range(2)])
    return (frac_out, vel_out, stress_out)
```

```python
import functools

import jax
import jax.numpy as jnp
from jax import lax
from jax.experimental import pallas as pl
from jax.experimental.pallas import tpu as pltpu
from jax.sharding import PartitionSpec as P

time_step = 0.05
gravity = 1.0
bulk_modulus = 4.0
mass_floor = 0.25
slip_floor = 0.25

F32 = jnp.float32
BF16 = jnp.bfloat16

WX, DX, MWX, CVX = 0, 6, 12, 18
YAT, WY, DY = 24, 25, 28
ZAT, WZ, DZ = 31, 32, 35
MVY, MVZ, STR = 38, 39, 40
PLANES = 41

GROUP = 8
WINDOW = 64
EDGE = 16


def spline(frac):
    r = frac - 0.5
    low, high = 0.5 - r, 0.5 + r
    w = (0.5 * low * low, 0.75 - r * r, 0.5 * high * high)
    d = ((-1.0 - r) * w[0], -r * w[1], (1.0 - r) * w[2])
    return w, d


def place(where_at, first, values):
    k = where_at - first
    out = jnp.where(k == 2.0, values[2], 0.0)
    out = jnp.where(k == 1.0, values[1], out)
    return jnp.where(k == 0.0, values[0], out)


def halves(value):
    high = value.astype(BF16)
    return high, (value - high.astype(F32)).astype(BF16)


def prepare(cell, frac, planes, moving=None):
    wx, dx = spline(frac[0])
    wy, dy = spline(frac[1])
    wz, dz = spline(frac[2])
    at_x = (cell // 16).astype(F32)
    at_y = (cell // 4 % 4).astype(F32)
    at_z = (cell % 4).astype(F32)
    planes[YAT] = at_y
    planes[ZAT] = at_z
    for t in range(3):
        planes[WY + t] = wy[t]
        planes[DY + t] = dy[t]
        planes[WZ + t] = wz[t]
        planes[DZ + t] = dz[t]
    if moving is not None:
        mass, vel, stress = moving
        scaled = (4.0 * time_step) * stress
        planes[MVY] = mass * vel[1]
        planes[MVZ] = mass * vel[2]
        planes[STR] = scaled
        mvx = mass * vel[0]
    for x in range(6):
        w = place(float(x), at_x, wx)
        d = place(float(x), at_x, dx)
        planes[WX + x] = w
        planes[DX + x] = d
        if moving is not None:
            planes[MWX + x] = mass * w
            planes[CVX + x] = mvx * w + scaled * d


def window_rows(q):
    first = EDGE + 4 * q - 1
    return 16 * (first // 16), 16 * ((first + 5) // 16 + 1)


def row_reader(planes, row, rows):
    return lambda k: planes[k, pl.ds(row, rows, stride=0), :]


def y_weights(get, yb):
    at = lax.broadcasted_iota(jnp.int32, (8, 128), 0).astype(F32)
    first = get(YAT) + (4.0 * yb - 1.0)
    w = place(at, first, [get(WY + t) for t in range(3)])
    d = place(at, first, [get(DY + t) for t in range(3)])
    return w, d


def z_weights(planes, row, q):
    low, high = window_rows(q)
    get = lambda k: jnp.concatenate([planes[k, pl.ds(row, 8, stride=0), :]] * ((high - low) // 8), axis=0)
    at = lax.broadcasted_iota(jnp.int32, (high - low, 128), 0).astype(F32) + float(low)
    first = get(ZAT) + float(EDGE + 4 * q - 1)
    w = place(at, first, [get(WZ + t) for t in range(3)])
    d = place(at, first, [get(DZ + t) for t in range(3)])
    return low, high, w, d, get


def window_mask(h, shape):
    lane = lax.broadcasted_iota(jnp.int32, shape, len(shape) - 1)
    z = lane + (4 * GROUP * h - EDGE)
    return (lane < WINDOW) & (z >= 0) & (z < 128)


def deposit(planes, left, right, out, nby, nbz):
    out[...] = jnp.zeros_like(out)

    def group(h, carry):
        for yb in range(nby):
            for q in range(GROUP):
                row = yb * nbz + h * GROUP + q
                get = row_reader(planes, row, 8)
                col = pl.ds((yb * GROUP + q) * 128, 128)
                wy, dy = y_weights(get, yb)
                by = get(MVY) * wy + get(STR) * dy
                parts = [get(MWX + x) * wy for x in range(6)]
                parts += [get(CVX + x) * wy for x in range(6)]
                wx = [get(WX + x) for x in range(6)]
                parts += [w * by for w in wx]
                parts += [w * wy for w in wx]
                a = jnp.concatenate(parts, axis=0)
                high, low = halves(a)
                left[0:192, col] = high
                left[192:384, col] = low
                first, last, wz, dz, zget = z_weights(planes, row, q)
                bz = zget(MVZ) * wz + zget(STR) * dz
                for k, value in enumerate(halves(wz) + halves(bz)):
                    right[k * WINDOW + first : k * WINDOW + last, col] = value
        o = lax.dot_general(left[...], right[...], (((1,), (1,)), ((), ())), preferred_element_type=F32)
        o = o[0:192] + o[192:384]
        o = jnp.concatenate([o[0:144, 0:128], o[144:192, 128:256]], axis=0)
        o = o + pltpu.roll(o, WINDOW, 1)
        o = jnp.where(window_mask(h, o.shape), o, 0.0)
        o = pltpu.roll(o, lax.rem(4 * GROUP * h + 128 - EDGE, 128), 1)
        out[...] += o.reshape(out.shape)
        return carry

    lax.fori_loop(0, nbz // GROUP, group, 0)


def gather(planes, vel, spread, sampled, right_w, right_d, nby, nbz):
    def group(h, carry):
        v = vel[...].reshape(144, 128)
        v = pltpu.roll(v, lax.rem(256 + EDGE - 4 * GROUP * h, 128), 1)
        v = jnp.where(window_mask(h, v.shape), v, 0.0)
        high = v.astype(BF16).astype(F32)
        v = (high + pltpu.roll(v - high, WINDOW, 1)).astype(BF16)
        v = jnp.concatenate([v, v], axis=1)
        for yb in range(nby):
            for q in range(GROUP):
                row = yb * nbz + h * GROUP + q
                col = pl.ds((yb * GROUP + q) * 128, 128)
                first, last, wz, dz, _ = z_weights(planes, row, q)
                for right, value in ((right_w, wz), (right_d, dz)):
                    hi, lo = halves(value)
                    for k, part in enumerate((hi, hi, lo, lo)):
                        right[k * WINDOW + first : k * WINDOW + last, col] = part
        spread[0:144] = jnp.dot(v, right_w[...], preferred_element_type=F32)
        spread[144:192] = jnp.dot(v[96:144], right_d[...], preferred_element_type=F32)
        for yb in range(nby):
            for q in range(GROUP):
                row = yb * nbz + h * GROUP + q
                get = row_reader(planes, row, 8)
                col = pl.ds((yb * GROUP + q) * 128, 128)
                wy, dy = y_weights(get, yb)
                wx = [get(WX + x) for x in range(6)]
                dx = [get(DX + x) for x in range(6)]
                read = lambda c, x: spread[48 * c + 8 * x : 48 * c + 8 * x + 8, col]
                vx, ax, vy, vz, az = (0.0,) * 5
                for x in range(6):
                    sx = read(0, x)
                    vx = vx + wx[x] * sx
                    ax = ax + dx[x] * sx
                    vy = vy + wx[x] * read(1, x)
                    vz = vz + wx[x] * read(2, x)
                    az = az + wx[x] * read(3, x)
                rows = (vx * wy, vy * wy, vz * wy, (ax + az) * wy + vy * dy)
                for k, value in enumerate(rows):
                    sampled[k, pl.ds(row, 1), :] = jnp.sum(value, axis=0, keepdims=True)
        return carry

    lax.fori_loop(0, nbz // GROUP, group, 0)


def node_velocity(fields):
    mass = fields[0]
    inverse = 1.0 / jnp.maximum(mass, mass_floor)
    vel = [fields[k] * inverse for k in (1, 2, 3)]
    lifted = vel[2] - time_step * gravity
    floor = lax.broadcasted_iota(jnp.int32, lifted.shape, 2) == 0
    vel[2] = jnp.where(floor, jnp.maximum(lifted, 0.0), lifted)
    return mass, vel


def dragged(mass, vel, other_mass, other_vel, coef):
    slip = [b - a for a, b in zip(vel, other_vel)]
    rate = coef * jnp.sqrt(slip[0] * slip[0] + slip[1] * slip[1] + slip[2] * slip[2] + slip_floor)
    share = rate / (1.0 + rate) * (other_mass / (mass + other_mass + mass_floor))
    return [a + share * s for a, s in zip(vel, slip)]


def store_masked(vel, nodes, has_left, has_right):
    layer = lax.broadcasted_iota(jnp.int32, vel[0].shape, 0)
    keep = ((layer > 0) | has_left) & ((layer < 5) | has_right)
    for k in range(3):
        nodes[k] = jnp.where(keep, vel[k], 0.0)


def sum_layers(own, from_left, from_right):
    own = own[...]
    return jnp.concatenate(
        [own[:, 0:2] + from_left, own[:, 2:4], own[:, 4:6] + from_right], axis=1
    )


def live_mask(count_ref, shape):
    return lax.broadcasted_iota(jnp.int32, shape, 1) < count_ref[...]


def advance(sampled, live, frac_ref, vel_ref, stress_ref):
    frac = [jnp.where(live, frac_ref[k] + time_step * sampled[k], frac_ref[k]) for k in range(3)]
    vel = [jnp.where(live, sampled[k], vel_ref[k]) for k in range(3)]
    old = stress_ref[...]
    stress = jnp.where(live, old - (time_step * bulk_modulus * 4.0) * sampled[3], old)
    return frac, vel, stress


def write_sends(dep, send_left, send_right):
    for c in range(4):
        for k in range(2):
            send_left[2 * c + k] = dep[c, k]
            send_right[2 * c + k] = dep[c, 4 + k]


def first_kernel(nby, nbz, cell, count, frac, vel, mass, stress, coef, dep, send_left, send_right, planes, left, right):
    live = live_mask(count, cell.shape)
    m = jnp.where(live, mass[...], 0.0)
    s = jnp.where(live, stress[...], 0.0)
    right[...] = jnp.zeros_like(right)
    prepare(cell[...], [frac[k] for k in range(3)], planes, (m, [vel[k] for k in range(3)], s))
    deposit(planes, left, right, dep, nby, nbz)
    write_sends(dep, send_left, send_right)
    send_left[8] = coef[0]
    send_right[8] = coef[3]


def sum_kernel(dep, from_left, from_right, fields):
    fields[...] = sum_layers(dep, from_left[0:8].reshape(4, 2, 8, 128), from_right[0:8].reshape(4, 2, 8, 128))


def middle_kernel(nby, nbz, cell, count, frac, vel, mass, stress, coef, fields, other, from_left, from_right,
                  new_frac, new_vel, new_stress, dep, send_left, send_right,
                  planes, left, right, right_w, right_d, spread, sampled, nodes):
    place_id, places = lax.axis_index("space"), lax.axis_size("space")
    right_w[...] = jnp.zeros_like(right_w)
    right_d[...] = jnp.zeros_like(right_d)
    right[...] = jnp.zeros_like(right)
    own_mass, own_vel = node_velocity(fields)
    other_mass, other_vel = node_velocity(other)
    coefs = jnp.concatenate([from_left[8:9], coef[...], from_right[8:9]], axis=0)
    own_vel = dragged(own_mass, own_vel, other_mass, other_vel, coefs)
    store_masked(own_vel, nodes, place_id > 0, place_id < places - 1)
    prepare(cell[...], [frac[k] for k in range(3)], planes)
    gather(planes, nodes, spread, sampled, right_w, right_d, nby, nbz)
    live = live_mask(count, cell.shape)
    f, v, t = advance(sampled, live, frac, vel, stress)
    for k in range(3):
        new_frac[k] = f[k]
        new_vel[k] = v[k]
    new_stress[...] = t
    m = jnp.where(live, mass[...], 0.0)
    s = jnp.where(live, t, 0.0)
    prepare(cell[...], f, planes, (m, v, s))
    deposit(planes, left, right, dep, nby, nbz)
    write_sends(dep, send_left, send_right)


def last_kernel(nby, nbz, cell, count, frac, vel, stress, dep, from_left, from_right,
                new_frac, new_vel, new_stress,
                planes, right_w, right_d, spread, sampled, nodes):
    place_id, places = lax.axis_index("space"), lax.axis_size("space")
    right_w[...] = jnp.zeros_like(right_w)
    right_d[...] = jnp.zeros_like(right_d)
    fields = sum_layers(dep, from_left[...].reshape(4, 2, 8, 128), from_right[...].reshape(4, 2, 8, 128))
    _, node_vel = node_velocity(fields)
    store_masked(node_vel, nodes, place_id > 0, place_id < places - 1)
    prepare(cell[...], [frac[k] for k in range(3)], planes)
    gather(planes, nodes, spread, sampled, right_w, right_d, nby, nbz)
    live = live_mask(count, cell.shape)
    f, v, t = advance(sampled, live, frac, vel, stress)
    for k in range(3):
        new_frac[k] = f[k]
        new_vel[k] = v[k]
    new_stress[...] = t


def call(kernel, name, outs, scratch, *args):
    vmem = pl.BlockSpec(memory_space=pltpu.VMEM)
    return pl.pallas_call(
        kernel,
        name=name,
        out_shape=[jax.ShapeDtypeStruct(s, F32) for s in outs],
        in_specs=[vmem] * len(args),
        out_specs=[vmem] * len(outs),
        scratch_shapes=scratch,
        compiler_params=pltpu.CompilerParams(vmem_limit_bytes=40 << 20),
    )(*args)


def local(particle_cell, block_count, particle_frac, particle_vel, particle_mass, particle_stress, drag_coef):
    cell, count = particle_cell[0], block_count[0][:, None]
    frac, vel = particle_frac[0], particle_vel[0]
    mass, stress = particle_mass[0], particle_stress[0]
    layers, ny, nz = drag_coef.shape
    nby, nbz = ny // 4, nz // 4
    blocks, slots = cell.shape
    lanes = nby * GROUP * slots
    places = lax.axis_size("space")
    up = [(i, i + 1) for i in range(places - 1)]
    down = [(j, i) for i, j in up]
    swap = [(i, i ^ 1) for i in range(lax.axis_size("phase"))]

    particle = (blocks, slots)
    triple = (3,) + particle
    grid = (4, layers + 2, ny, nz)
    planes = pltpu.VMEM((PLANES,) + particle, F32)
    left = pltpu.VMEM((384, lanes), BF16)
    right = pltpu.VMEM((4 * WINDOW, lanes), BF16)
    spread = pltpu.VMEM((192, lanes), F32)
    sampled = pltpu.VMEM((4,) + particle, F32)
    nodes = pltpu.VMEM((3,) + grid[1:], F32)

    def exchange(send_left, send_right):
        return lax.ppermute(send_right, "space", up), lax.ppermute(send_left, "space", down)

    sent = (9, ny, nz)
    dep, send_left, send_right = call(
        functools.partial(first_kernel, nby, nbz), "first", [grid, sent, sent], [planes, left, right],
        cell, count, frac, vel, mass, stress, drag_coef)
    from_left, from_right = exchange(send_left, send_right)
    fields, = call(sum_kernel, "total", [grid], [], dep, from_left, from_right)
    other = lax.ppermute(fields, "phase", swap)
    sent = (8, ny, nz)
    frac, vel, stress, dep, send_left, send_right = call(
        functools.partial(middle_kernel, nby, nbz), "middle", [triple, triple, particle, grid, sent, sent],
        [planes, left, right, right, right, spread, sampled, nodes],
        cell, count, frac, vel, mass, stress, drag_coef, fields, other, from_left, from_right)
    from_left, from_right = exchange(send_left, send_right)
    frac, vel, stress = call(
        functools.partial(last_kernel, nby, nbz), "last", [triple, triple, particle],
        [planes, right, right, spread, sampled, nodes],
        cell, count, frac, vel, stress, dep, from_left, from_right)
    return frac[None], vel[None], stress[None]


def solution(mesh):
    in_specs = (
        P("phase", "space", None),
        P("phase", "space"),
        P("phase", None, "space", None),
        P("phase", None, "space", None),
        P("phase", "space", None),
        P("phase", "space", None),
        P("space", None, None),
    )
    out_specs = (
        P("phase", None, "space", None),
        P("phase", None, "space", None),
        P("phase", "space", None),
    )
    return jax.shard_map(local, mesh=mesh, in_specs=in_specs, out_specs=out_specs, check_vma=False)
```

```python
import functools

import jax
import jax.numpy as jnp
from jax import lax
from jax.experimental import pallas as pl
from jax.experimental.pallas import tpu as pltpu
from jax.sharding import PartitionSpec as P

time_step = 0.05
gravity = 1.0
bulk_modulus = 4.0
mass_floor = 0.25
slip_floor = 0.25

F32 = jnp.float32
BF16 = jnp.bfloat16

WX, DX, MWX, CVX = 0, 6, 12, 18
YAT, WY, DY = 24, 25, 28
ZAT, WZ, DZ = 31, 32, 35
MVY, MVZ, STR = 38, 39, 40
PLANES = 41

GROUP = 8
WINDOW = 64
EDGE = 1
OUTER = (0, 1, 4, 5)
INNER = (2, 3)
ALL = (0, 1, 2, 3, 4, 5)


def spline(frac):
    r = frac - 0.5
    low, high = 0.5 - r, 0.5 + r
    w = (0.5 * low * low, 0.75 - r * r, 0.5 * high * high)
    d = ((-1.0 - r) * w[0], -r * w[1], (1.0 - r) * w[2])
    return w, d


def place(where_at, first, values):
    k = where_at - first
    out = jnp.where(k == 2.0, values[2], 0.0)
    out = jnp.where(k == 1.0, values[1], out)
    return jnp.where(k == 0.0, values[0], out)


def halves(value):
    high = value.astype(BF16)
    return high, (value - high.astype(F32)).astype(BF16)


def prepare(cell, frac, planes, moving=None):
    wx, dx = spline(frac[0])
    wy, dy = spline(frac[1])
    wz, dz = spline(frac[2])
    at_x = (cell // 16).astype(F32)
    at_y = (cell // 4 % 4).astype(F32)
    at_z = (cell % 4).astype(F32)
    planes[YAT] = at_y
    planes[ZAT] = at_z
    for t in range(3):
        planes[WY + t] = wy[t]
        planes[DY + t] = dy[t]
        planes[WZ + t] = wz[t]
        planes[DZ + t] = dz[t]
    if moving is not None:
        mass, vel, stress = moving
        scaled = (4.0 * time_step) * stress
        planes[MVY] = mass * vel[1]
        planes[MVZ] = mass * vel[2]
        planes[STR] = scaled
        mvx = mass * vel[0]
    for x in range(6):
        w = place(float(x), at_x, wx)
        d = place(float(x), at_x, dx)
        planes[WX + x] = w
        planes[DX + x] = d
        if moving is not None:
            planes[MWX + x] = mass * w
            planes[CVX + x] = mvx * w + scaled * d


def row_reader(planes, row, rows):
    return lambda k: planes[k, pl.ds(row, rows, stride=0), :]


def y_weights(get, yb):
    at = lax.broadcasted_iota(jnp.int32, (8, 128), 0).astype(F32)
    first = get(YAT) + (4.0 * yb - 1.0)
    w = place(at, first, [get(WY + t) for t in range(3)])
    d = place(at, first, [get(DY + t) for t in range(3)])
    return w, d


def z_weights(planes, row, q, others):
    low, high = 4 * q // 8 * 8, (4 * q + 5) // 8 * 8 + 8
    count = (high - low) // 8
    get = lambda k: jnp.concatenate([planes[k, pl.ds(row, 8, stride=0), :]] * count, axis=0)
    at = lax.broadcasted_iota(jnp.int32, (high - low, 128), 0).astype(F32)
    first = get(ZAT) + float(4 * q - low)
    w = place(at, first, [get(WZ + t) for t in range(3)])
    d = place(at, first, [get(DZ + t) for t in range(3)])
    first, last = low // 16 * 16, -(-high // 16) * 16
    tiles = []
    for value in (w, others(get, w, d)):
        zeros = lambda n: [jnp.zeros((n, 128), F32)] if n else []
        value = jnp.concatenate(zeros(low - first) + [value] + zeros(last - high), axis=0)
        tiles.append(halves(value))
    return first, last, tiles


def window_mask(h, shape):
    lane = lax.broadcasted_iota(jnp.int32, shape, len(shape) - 1)
    z = lane + (4 * GROUP * h - EDGE)
    return (lane < WINDOW) & (z >= 0) & (z < 128)


def deposit(planes, left, right, out, xs, nby, nbz):
    out[...] = jnp.zeros_like(out)
    n = len(xs)
    rows = 32 * n
    force = lambda get, w, d: get(MVZ) * w + get(STR) * d

    def group(h, carry):
        for yb in range(nby):
            for q in range(GROUP):
                row = yb * nbz + h * GROUP + q
                get = row_reader(planes, row, 8)
                col = pl.ds((yb * GROUP + q) * 128, 128)
                wy, dy = y_weights(get, yb)
                by = get(MVY) * wy + get(STR) * dy
                for k in range(0, n, 2):
                    pair = [get(WX + x) for x in xs[k : k + 2]]
                    for c, parts in enumerate((
                        [get(MWX + x) * wy for x in xs[k : k + 2]],
                        [get(CVX + x) * wy for x in xs[k : k + 2]],
                        [w * by for w in pair],
                        [w * wy for w in pair],
                    )):
                        high, low = halves(jnp.concatenate(parts, axis=0))
                        at = 8 * (n * c + k)
                        left[at : at + 16, col] = high
                        left[rows + at : rows + at + 16, col] = low
                first, last, tiles = z_weights(planes, row, q, force)
                for k, value in enumerate(tiles[0] + tiles[1]):
                    right[k * WINDOW + first : k * WINDOW + last, col] = value
        o = lax.dot_general(left[0 : 2 * rows], right[...], (((1,), (1,)), ((), ())), preferred_element_type=F32)
        o = o[0:rows] + o[rows : 2 * rows]
        o = jnp.concatenate([o[0 : 24 * n, 0:128], o[24 * n : rows, 128:256]], axis=0)
        o = o + pltpu.roll(o, WINDOW, 1)
        o = jnp.where(window_mask(h, o.shape), o, 0.0)
        o = pltpu.roll(o, lax.rem(4 * GROUP * h + 128 - EDGE, 128), 1)
        out[...] += o.reshape(out.shape)
        return carry

    lax.fori_loop(0, nbz // GROUP, group, 0)


def gather(planes, vel, spread, sampled, right_w, right_d, xs, nby, nbz):
    n = len(xs)
    slope = lambda get, w, d: d

    def group(h, carry):
        v = vel[...].reshape(24 * n, 128)
        v = pltpu.roll(v, lax.rem(256 + EDGE - 4 * GROUP * h, 128), 1)
        v = jnp.where(window_mask(h, v.shape), v, 0.0)
        high = v.astype(BF16).astype(F32)
        v = (high + pltpu.roll(v - high, WINDOW, 1)).astype(BF16)
        v = jnp.concatenate([v, v], axis=1)
        for yb in range(nby):
            for q in range(GROUP):
                row = yb * nbz + h * GROUP + q
                col = pl.ds((yb * GROUP + q) * 128, 128)
                first, last, tiles = z_weights(planes, row, q, slope)
                for right, (hi, lo) in zip((right_w, right_d), tiles):
                    for k, part in enumerate((hi, hi, lo, lo)):
                        right[k * WINDOW + first : k * WINDOW + last, col] = part
        spread[0 : 24 * n] = jnp.dot(v, right_w[...], preferred_element_type=F32)
        spread[24 * n : 32 * n] = jnp.dot(v[16 * n :], right_d[...], preferred_element_type=F32)
        for yb in range(nby):
            for q in range(GROUP):
                row = yb * nbz + h * GROUP + q
                get = row_reader(planes, row, 8)
                col = pl.ds((yb * GROUP + q) * 128, 128)
                wy, dy = y_weights(get, yb)
                read = lambda c, k: spread[8 * (n * c + k) : 8 * (n * c + k) + 8, col]
                vx, ax, vy, vz, az = (0.0,) * 5
                for k, x in enumerate(xs):
                    w, sx = get(WX + x), read(0, k)
                    vx = vx + w * sx
                    ax = ax + get(DX + x) * sx
                    vy = vy + w * read(1, k)
                    vz = vz + w * read(2, k)
                    az = az + w * read(3, k)
                for k, value in enumerate((vx * wy, vy * wy, vz * wy, (ax + az) * wy + vy * dy)):
                    sampled[k, pl.ds(row, 1), :] = jnp.sum(value, axis=0, keepdims=True)
        return carry

    lax.fori_loop(0, nbz // GROUP, group, 0)


def node_velocity(fields):
    mass = fields[0]
    inverse = 1.0 / jnp.maximum(mass, mass_floor)
    vel = [fields[k] * inverse for k in (1, 2, 3)]
    lifted = vel[2] - time_step * gravity
    floor = lax.broadcasted_iota(jnp.int32, lifted.shape, 2) == 0
    vel[2] = jnp.where(floor, jnp.maximum(lifted, 0.0), lifted)
    return mass, vel


def dragged(mass, vel, other_mass, other_vel, coef):
    slip = [b - a for a, b in zip(vel, other_vel)]
    rate = coef * jnp.sqrt(slip[0] * slip[0] + slip[1] * slip[1] + slip[2] * slip[2] + slip_floor)
    share = rate / (1.0 + rate) * (other_mass / (mass + other_mass + mass_floor))
    return [a + share * s for a, s in zip(vel, slip)]


class Side:
    def __init__(self):
        place_id = lax.axis_index("space")
        self.even = lax.rem(place_id, 2) == 0
        self.has_left = place_id > 0
        self.has_right = place_id < lax.axis_size("space") - 1

    def arrived(self, first, second, rows):
        first, second = first[rows], second[rows]
        from_left = jnp.where(self.even, second, first)
        from_right = jnp.where(self.even, first, second)
        return jnp.where(self.has_left, from_left, 0.0), jnp.where(self.has_right, from_right, 0.0)

    def layers(self, outer, first, second):
        left, right = self.arrived(first, second, slice(0, 8))
        shape = (4, 2) + left.shape[1:]
        outer = outer[...]
        return outer[:, 0:2] + left.reshape(shape), outer[:, 2:4] + right.reshape(shape)

    def send(self, outer, first, second, coef=None):
        toward = jnp.where(self.even, 2, 0)
        for ref, start in ((first, toward), (second, 2 - toward)):
            for c in range(4):
                ref[2 * c : 2 * c + 2] = outer[c, pl.ds(start, 2)]
        if coef is not None:
            first[8] = jnp.where(self.even, coef[3], coef[0])
            second[8] = jnp.where(self.even, coef[0], coef[3])

    def keep(self, vel):
        layer = lax.broadcasted_iota(jnp.int32, vel.shape, 0)
        keep = ((layer > 0) | self.has_left) & ((layer < vel.shape[0] - 1) | self.has_right)
        return jnp.where(keep, vel, 0.0)


def live_mask(count, shape):
    return lax.broadcasted_iota(jnp.int32, shape, 1) < count[...]


def advance(sampled, live, frac_ref, vel_ref, stress_ref):
    frac = [jnp.where(live, frac_ref[k] + time_step * sampled[k], frac_ref[k]) for k in range(3)]
    vel = [jnp.where(live, sampled[k], vel_ref[k]) for k in range(3)]
    old = stress_ref[...]
    stress = jnp.where(live, old - (time_step * bulk_modulus * 4.0) * sampled[3], old)
    return frac, vel, stress


def store_state(state, new_frac, new_vel, new_stress):
    frac, vel, stress = state
    for k in range(3):
        new_frac[k] = frac[k]
        new_vel[k] = vel[k]
    new_stress[...] = stress


def first_kernel(nby, nbz, *refs):
    sources, (planes, outer, first, second), rest = refs[:7], refs[7:11], refs[11:]
    inputs, (left, right, sems) = rest[:7], rest[7:]
    copies = [pltpu.make_async_copy(a, b, sems.at[k]) for k, (a, b) in enumerate(zip(sources, inputs))]
    for copy in copies:
        copy.start()
    right[...] = jnp.zeros_like(right)
    for copy in copies:
        copy.wait()
    cell, count, frac, vel, mass, stress, coef = inputs
    live = live_mask(count, cell.shape)
    m = jnp.where(live, mass[...], 0.0)
    s = jnp.where(live, stress[...], 0.0)
    prepare(cell[...], [frac[k] for k in range(3)], planes, (m, [vel[k] for k in range(3)], s))
    deposit(planes, left, right, outer, OUTER, nby, nbz)
    Side().send(outer, first, second, coef)


def inner_kernel(nby, nbz, planes, inner, left, right):
    right[...] = jnp.zeros_like(right)
    deposit(planes, left, right, inner, INNER, nby, nbz)


def total_kernel(outer, inner, first, second, fields):
    low, high = Side().layers(outer, first, second)
    fields[:, 0:2] = low
    fields[:, 2:4] = inner[...]
    fields[:, 4:6] = high


def middle_kernel(nby, nbz, cell, count, frac, vel, mass, stress, coef, planes, fields, other, first, second,
                  new_frac, new_vel, new_stress, new_planes, outer, new_first, new_second,
                  left, right_w, right_d, spread, sampled, nodes):
    side = Side()
    right_w[...] = jnp.zeros_like(right_w)
    right_d[...] = jnp.zeros_like(right_d)
    own_mass, own_vel = node_velocity(fields)
    other_mass, other_vel = node_velocity(other)
    low, high = side.arrived(first, second, slice(8, 9))
    coefs = jnp.concatenate([low, coef[...], high], axis=0)
    for k, v in enumerate(dragged(own_mass, own_vel, other_mass, other_vel, coefs)):
        nodes[k] = side.keep(v)
    gather(planes, nodes, spread, sampled, right_w, right_d, ALL, nby, nbz)
    live = live_mask(count, cell.shape)
    state = advance(sampled, live, frac, vel, stress)
    store_state(state, new_frac, new_vel, new_stress)
    m = jnp.where(live, mass[...], 0.0)
    s = jnp.where(live, state[2], 0.0)
    prepare(cell[...], state[0], new_planes, (m, state[1], s))
    deposit(new_planes, left, right_w, outer, OUTER, nby, nbz)
    side.send(outer, new_first, new_second)


def inner_pass_kernel(nby, nbz, planes, sampled, inner, left, right_w, right_d, spread, nodes):
    right_w[...] = jnp.zeros_like(right_w)
    right_d[...] = jnp.zeros_like(right_d)
    deposit(planes, left, right_w, inner, INNER, nby, nbz)
    _, vel = node_velocity(inner)
    for k in range(3):
        nodes[k] = vel[k]
    gather(planes, nodes, spread, sampled, right_w, right_d, INNER, nby, nbz)


def last_kernel(nby, nbz, cell, count, frac, vel, stress, planes, partial, outer, first, second,
                new_frac, new_vel, new_stress, right_w, right_d, spread, sampled, nodes):
    side = Side()
    right_w[...] = jnp.zeros_like(right_w)
    right_d[...] = jnp.zeros_like(right_d)
    low, high = side.layers(outer, first, second)
    _, node_vel = node_velocity(jnp.concatenate([low, high], axis=1))
    for k in range(3):
        nodes[k] = side.keep(node_vel[k])
    gather(planes, nodes, spread, sampled, right_w, right_d, OUTER, nby, nbz)
    sampled[...] += partial[...]
    live = live_mask(count, cell.shape)
    store_state(advance(sampled, live, frac, vel, stress), new_frac, new_vel, new_stress)


def call(kernel, name, outs, scratch, *args, space=pltpu.VMEM, cost=None, limit=24 << 20):
    spec = pl.BlockSpec(memory_space=space)
    vmem = pl.BlockSpec(memory_space=pltpu.VMEM)
    return pl.pallas_call(
        kernel,
        name=name,
        out_shape=[jax.ShapeDtypeStruct(s, F32) for s in outs],
        in_specs=[spec] * len(args),
        out_specs=[vmem] * len(outs),
        scratch_shapes=scratch,
        cost_estimate=cost,
        compiler_params=pltpu.CompilerParams(vmem_limit_bytes=limit),
    )(*args)


def local(particle_cell, block_count, particle_frac, particle_vel, particle_mass, particle_stress, drag_coef):
    cell, count = particle_cell[0], block_count[0][:, None]
    frac, vel = particle_frac[0], particle_vel[0]
    mass, stress = particle_mass[0], particle_stress[0]
    _, ny, nz = drag_coef.shape
    sizes = nby, nbz = ny // 4, nz // 4
    blocks, slots = cell.shape
    lanes = nby * GROUP * slots
    places = lax.axis_size("space")

    def matching(start):
        pairs = [(i, i) for i in range(start)]
        for i in range(start, places - 1, 2):
            pairs += [(i, i + 1), (i + 1, i)]
        return pairs + [(i, i) for i in range(len(pairs), places)]

    swap = [(i, i ^ 1) for i in range(lax.axis_size("phase"))]
    particle = (blocks, slots)
    triple = (3,) + particle
    layers = lambda channels, n: (channels, n, ny, nz)
    planes_shape = (PLANES,) + particle
    left = lambda n: pltpu.VMEM((64 * n, lanes), BF16)
    right = pltpu.VMEM((4 * WINDOW, lanes), BF16)
    spread = lambda n: pltpu.VMEM((32 * n, lanes), F32)
    nodes = lambda n: pltpu.VMEM(layers(3, n), F32)
    sampled = pltpu.VMEM((4,) + particle, F32)
    cost = pl.CostEstimate(flops=3 << 30, bytes_accessed=1 << 20, transcendentals=0)

    def exchange(first, second):
        second = lax.ppermute(second, "space", matching(1))
        return lax.ppermute(first, "space", matching(0)), second

    inputs = (cell, count, frac, vel, mass, stress, drag_coef)
    sent = (9, ny, nz)
    planes, outer, first, second = call(
        functools.partial(first_kernel, *sizes), "first", [planes_shape, layers(4, 4), sent, sent],
        [pltpu.VMEM(a.shape, a.dtype) for a in inputs] + [left(4), right, pltpu.SemaphoreType.DMA((7,))],
        *[pltpu.with_memory_space_constraint(a, pltpu.HBM) for a in inputs], space=pltpu.HBM)
    first, second = exchange(first, second)
    inner, = call(functools.partial(inner_kernel, *sizes), "inner", [layers(4, 2)], [left(2), right],
                  planes, cost=cost)
    fields, = call(total_kernel, "total", [layers(4, 6)], [], outer, inner, first, second)
    other = lax.ppermute(fields, "phase", swap)
    sent = (8, ny, nz)
    frac, vel, stress, planes, outer, first, second = call(
        functools.partial(middle_kernel, *sizes), "middle",
        [triple, triple, particle, planes_shape, layers(4, 4), sent, sent],
        [left(4), right, right, spread(6), sampled, nodes(6)],
        *inputs, planes, fields, other, first, second)
    first, second = exchange(first, second)
    partial, _ = call(functools.partial(inner_pass_kernel, *sizes), "inner_pass",
                      [(4,) + particle, layers(4, 2)], [left(2), right, right, spread(2), nodes(2)],
                      planes, cost=cost)
    frac, vel, stress = call(
        functools.partial(last_kernel, *sizes), "last", [triple, triple, particle],
        [right, right, spread(4), sampled, nodes(4)],
        cell, count, frac, vel, stress, planes, partial, outer, first, second)
    return frac[None], vel[None], stress[None]


def solution(mesh):
    in_specs = (
        P("phase", "space", None),
        P("phase", "space"),
        P("phase", None, "space", None),
        P("phase", None, "space", None),
        P("phase", "space", None),
        P("phase", "space", None),
        P("space", None, None),
    )
    out_specs = (
        P("phase", None, "space", None),
        P("phase", None, "space", None),
        P("phase", "space", None),
    )
    return jax.shard_map(local, mesh=mesh, in_specs=in_specs, out_specs=out_specs, check_vma=False)
```

```python
import functools

import jax
import jax.numpy as jnp
from jax import lax
from jax.experimental import pallas as pl
from jax.experimental.pallas import tpu as pltpu
from jax.sharding import PartitionSpec as P

time_step = 0.05
gravity = 1.0
bulk_modulus = 4.0
mass_floor = 0.25
slip_floor = 0.25

F32 = jnp.float32
BF16 = jnp.bfloat16

WX, DX, MWX, CVX = 0, 6, 12, 18
YAT, WY, DY = 24, 25, 28
ZAT, WZ, DZ = 31, 32, 35
MVY, MVZ, STR, LIVE = 38, 39, 40, 41
PLANES = 42

GROUP = 8
WINDOW = 64
EDGE = 1
OUTER = (0, 1, 4, 5)
INNER = (2, 3)
ALL = (0, 1, 2, 3, 4, 5)


def spline(frac):
    r = frac - 0.5
    low, high = 0.5 - r, 0.5 + r
    w = (0.5 * low * low, 0.75 - r * r, 0.5 * high * high)
    d = ((-1.0 - r) * w[0], -r * w[1], (1.0 - r) * w[2])
    return w, d


def place(where_at, first, values):
    k = where_at - first
    out = jnp.where(k == 2.0, values[2], 0.0)
    out = jnp.where(k == 1.0, values[1], out)
    return jnp.where(k == 0.0, values[0], out)


def halves(value):
    high = value.astype(BF16)
    return high, (value - high.astype(F32)).astype(BF16)


def prepare(cell, frac, planes, moving=None):
    wx, dx = spline(frac[0])
    wy, dy = spline(frac[1])
    wz, dz = spline(frac[2])
    at_x = (cell >> 4).astype(F32)
    at_y = ((cell >> 2) & 3).astype(F32)
    at_z = (cell & 3).astype(F32)
    planes[YAT] = at_y
    planes[ZAT] = at_z
    for t in range(3):
        planes[WY + t] = wy[t]
        planes[DY + t] = dy[t]
        planes[WZ + t] = wz[t]
        planes[DZ + t] = dz[t]
    if moving is not None:
        mass, vel, stress = moving
        scaled = (4.0 * time_step) * stress
        planes[MVY] = mass * vel[1]
        planes[MVZ] = mass * vel[2]
        planes[STR] = scaled
        mvx = mass * vel[0]
    for x in range(6):
        w = place(float(x), at_x, wx)
        d = place(float(x), at_x, dx)
        planes[WX + x] = w
        planes[DX + x] = d
        if moving is not None:
            planes[MWX + x] = mass * w
            planes[CVX + x] = mvx * w + scaled * d


def row_reader(planes, row, rows):
    return lambda k: planes[k, pl.ds(row, rows, stride=0), :]


def y_weights(get, yb):
    at = lax.broadcasted_iota(jnp.int32, (8, 128), 0).astype(F32)
    first = get(YAT) + (4.0 * yb - 1.0)
    w = place(at, first, [get(WY + t) for t in range(3)])
    d = place(at, first, [get(DY + t) for t in range(3)])
    return w, d


def z_tiles(q):
    low, high = 4 * q // 8 * 8, (4 * q + 5) // 8 * 8 + 8
    return low, high, low // 16 * 16, -(-high // 16) * 16


def clear(ref):
    for b in range(ref.shape[0]):
        _, _, first, last = z_tiles(b % GROUP)
        for k in range(4):
            for row in range(0, WINDOW, 16):
                if not first <= row < last:
                    ref[b, k * WINDOW + row : k * WINDOW + row + 16] = jnp.zeros((16, 128), F32).astype(BF16)


def z_weights(planes, row, q, others):
    low, high, start, stop = z_tiles(q)
    count = (high - low) // 8
    get = lambda k: jnp.concatenate([planes[k, pl.ds(row, 8, stride=0), :]] * count, axis=0)
    at = lax.broadcasted_iota(jnp.int32, (high - low, 128), 0).astype(F32)
    first = get(ZAT) + float(4 * q - low)
    w = place(at, first, [get(WZ + t) for t in range(3)])
    d = place(at, first, [get(DZ + t) for t in range(3)])
    tiles = []
    for value in (w, others(get, w, d)):
        zeros = lambda n: [jnp.zeros((n, 128), F32)] if n else []
        value = jnp.concatenate(zeros(low - start) + [value] + zeros(stop - high), axis=0)
        tiles.append(halves(value))
    return start, stop, tiles


def side_by_side(ref, rows):
    return jnp.concatenate([ref[b, 0:rows] for b in range(ref.shape[0])], axis=1)


def window_mask(h, shape):
    lane = lax.broadcasted_iota(jnp.int32, shape, len(shape) - 1)
    z = lane + (4 * GROUP * h - EDGE)
    return (lane < WINDOW) & (z >= 0) & (z < 128)


def deposit(planes, left, right, out, xs, nby, nbz):
    out[...] = jnp.zeros_like(out)
    n = len(xs)
    rows = 32 * n
    force = lambda get, w, d: get(MVZ) * w + get(STR) * d

    def group(h, carry):
        for yb in range(nby):
            for q in range(GROUP):
                row = yb * nbz + h * GROUP + q
                get = row_reader(planes, row, 8)
                b = yb * GROUP + q
                wy, dy = y_weights(get, yb)
                by = get(MVY) * wy + get(STR) * dy
                for k in range(0, n, 2):
                    pair = [get(WX + x) for x in xs[k : k + 2]]
                    for c, parts in enumerate((
                        [get(MWX + x) * wy for x in xs[k : k + 2]],
                        [get(CVX + x) * wy for x in xs[k : k + 2]],
                        [w * by for w in pair],
                        [w * wy for w in pair],
                    )):
                        high, low = halves(jnp.concatenate(parts, axis=0))
                        at = 8 * (n * c + k)
                        left[b, at : at + 16] = high
                        left[b, rows + at : rows + at + 16] = low
                first, last, tiles = z_weights(planes, row, q, force)
                for k, value in enumerate(tiles[0] + tiles[1]):
                    right[b, k * WINDOW + first : k * WINDOW + last] = value
        o = lax.dot_general(side_by_side(left, 2 * rows), side_by_side(right, 4 * WINDOW), (((1,), (1,)), ((), ())), preferred_element_type=F32)
        o = o[0:rows] + o[rows : 2 * rows]
        o = jnp.concatenate([o[0 : 24 * n, 0:128], o[24 * n : rows, 128:256]], axis=0)
        o = o + pltpu.roll(o, WINDOW, 1)
        o = jnp.where(window_mask(h, o.shape), o, 0.0)
        o = pltpu.roll(o, lax.rem(4 * GROUP * h + 128 - EDGE, 128), 1)
        out[...] += o.reshape(out.shape)
        return carry

    lax.fori_loop(0, nbz // GROUP, group, 0)


def gather(planes, vel, spread, sampled, right_w, right_d, xs, nby, nbz):
    n = len(xs)
    slope = lambda get, w, d: d

    def group(h, carry):
        v = vel[...].reshape(24 * n, 128)
        v = pltpu.roll(v, lax.rem(256 + EDGE - 4 * GROUP * h, 128), 1)
        v = jnp.where(window_mask(h, v.shape), v, 0.0)
        high = v.astype(BF16).astype(F32)
        v = (high + pltpu.roll(v - high, WINDOW, 1)).astype(BF16)
        v = jnp.concatenate([v, v], axis=1)
        for yb in range(nby):
            for q in range(GROUP):
                row = yb * nbz + h * GROUP + q
                b = yb * GROUP + q
                first, last, tiles = z_weights(planes, row, q, slope)
                for right, (hi, lo) in zip((right_w, right_d), tiles):
                    for k, part in enumerate((hi, hi, lo, lo)):
                        right[b, k * WINDOW + first : k * WINDOW + last] = part
        spread[0 : 24 * n] = jnp.dot(v, side_by_side(right_w, 4 * WINDOW), preferred_element_type=F32)
        spread[24 * n : 32 * n] = jnp.dot(v[16 * n :], side_by_side(right_d, 4 * WINDOW), preferred_element_type=F32)
        for yb in range(nby):
            for q in range(GROUP):
                row = yb * nbz + h * GROUP + q
                get = row_reader(planes, row, 8)
                col = pl.ds((yb * GROUP + q) * 128, 128)
                wy, dy = y_weights(get, yb)
                read = lambda c, k: spread[8 * (n * c + k) : 8 * (n * c + k) + 8, col]
                vx, ax, vy, vz, az = (0.0,) * 5
                for k, x in enumerate(xs):
                    w, sx = get(WX + x), read(0, k)
                    vx = vx + w * sx
                    ax = ax + get(DX + x) * sx
                    vy = vy + w * read(1, k)
                    vz = vz + w * read(2, k)
                    az = az + w * read(3, k)
                for k, value in enumerate((vx * wy, vy * wy, vz * wy, (ax + az) * wy + vy * dy)):
                    sampled[k, pl.ds(row, 1), :] = jnp.sum(value, axis=0, keepdims=True)
        return carry

    lax.fori_loop(0, nbz // GROUP, group, 0)


def node_velocity(fields):
    mass = fields[0]
    inverse = 1.0 / jnp.maximum(mass, mass_floor)
    vel = [fields[k] * inverse for k in (1, 2, 3)]
    lifted = vel[2] - time_step * gravity
    floor = lax.broadcasted_iota(jnp.int32, lifted.shape, 2) == 0
    vel[2] = jnp.where(floor, jnp.maximum(lifted, 0.0), lifted)
    return mass, vel


def dragged(mass, vel, other_mass, other_vel, coef):
    slip = [b - a for a, b in zip(vel, other_vel)]
    rate = coef * jnp.sqrt(slip[0] * slip[0] + slip[1] * slip[1] + slip[2] * slip[2] + slip_floor)
    share = rate / (1.0 + rate) * (other_mass / (mass + other_mass + mass_floor))
    return [a + share * s for a, s in zip(vel, slip)]


class Side:
    def __init__(self):
        place_id = lax.axis_index("space")
        self.even = lax.rem(place_id, 2) == 0
        self.has_left = place_id > 0
        self.has_right = place_id < lax.axis_size("space") - 1

    def arrived(self, first, second, rows):
        first, second = first[rows], second[rows]
        from_left = jnp.where(self.even, second, first)
        from_right = jnp.where(self.even, first, second)
        return jnp.where(self.has_left, from_left, 0.0), jnp.where(self.has_right, from_right, 0.0)

    def layers(self, outer, first, second):
        left, right = self.arrived(first, second, slice(0, 8))
        shape = (4, 2) + left.shape[1:]
        outer = outer[...]
        return outer[:, 0:2] + left.reshape(shape), outer[:, 2:4] + right.reshape(shape)

    def send(self, outer, first, second, coef=None):
        toward = jnp.where(self.even, 2, 0)
        for ref, start in ((first, toward), (second, 2 - toward)):
            for c in range(4):
                ref[2 * c : 2 * c + 2] = outer[c, pl.ds(start, 2)]
        if coef is not None:
            first[8] = jnp.where(self.even, coef[3], coef[0])
            second[8] = jnp.where(self.even, coef[0], coef[3])

    def keep(self, vel):
        layer = lax.broadcasted_iota(jnp.int32, vel.shape, 0)
        keep = ((layer > 0) | self.has_left) & ((layer < vel.shape[0] - 1) | self.has_right)
        return jnp.where(keep, vel, 0.0)


def live_mask(count, shape):
    square = (shape[0], shape[0])
    same = lax.broadcasted_iota(jnp.int32, square, 0) == lax.broadcasted_iota(jnp.int32, square, 1)
    column = jnp.sum(jnp.where(same, count[...].astype(F32), 0.0), axis=1, keepdims=True)
    return lax.broadcasted_iota(jnp.int32, shape, 1).astype(F32) < column


def advance(sampled, live, frac_ref, vel_ref, stress_ref):
    frac = [jnp.where(live, frac_ref[k] + time_step * sampled[k], frac_ref[k]) for k in range(3)]
    vel = [jnp.where(live, sampled[k], vel_ref[k]) for k in range(3)]
    old = stress_ref[...]
    stress = jnp.where(live, old - (time_step * bulk_modulus * 4.0) * sampled[3], old)
    return frac, vel, stress


def store_state(state, new_frac, new_vel, new_stress):
    frac, vel, stress = state
    for k in range(3):
        new_frac[k] = frac[k]
        new_vel[k] = vel[k]
    new_stress[...] = stress


def first_kernel(nby, nbz, *refs):
    sources, (planes, outer, first, second), rest = refs[:7], refs[7:11], refs[11:]
    inputs, (left, right, sems) = rest[:7], rest[7:]
    copies = [pltpu.make_async_copy(a, b, sems.at[k]) for k, (a, b) in enumerate(zip(sources, inputs))]
    for copy in copies:
        copy.start()
    clear(right)
    for copy in copies:
        copy.wait()
    cell, count, frac, vel, mass, stress, coef = inputs
    live = live_mask(count, cell.shape)
    planes[LIVE] = jnp.where(live, 1.0, 0.0)
    m = jnp.where(live, mass[...], 0.0)
    s = jnp.where(live, stress[...], 0.0)
    prepare(cell[...], [frac[k] for k in range(3)], planes, (m, [vel[k] for k in range(3)], s))
    deposit(planes, left, right, outer, OUTER, nby, nbz)
    Side().send(outer, first, second, coef)


def inner_kernel(nby, nbz, planes, inner, left, right):
    clear(right)
    deposit(planes, left, right, inner, INNER, nby, nbz)


def total_kernel(outer, inner, first, second, fields):
    low, high = Side().layers(outer, first, second)
    fields[:, 0:2] = low
    fields[:, 2:4] = inner[...]
    fields[:, 4:6] = high


def middle_kernel(nby, nbz, cell, frac, vel, mass, stress, coef, planes, fields, other, first, second,
                  new_frac, new_vel, new_stress, new_planes, outer, new_first, new_second,
                  left, right_w, right_d, spread, sampled, nodes):
    side = Side()
    clear(right_w)
    clear(right_d)
    own_mass, own_vel = node_velocity(fields)
    other_mass, other_vel = node_velocity(other)
    low, high = side.arrived(first, second, slice(8, 9))
    coefs = jnp.concatenate([low, coef[...], high], axis=0)
    for k, v in enumerate(dragged(own_mass, own_vel, other_mass, other_vel, coefs)):
        nodes[k] = side.keep(v)
    gather(planes, nodes, spread, sampled, right_w, right_d, ALL, nby, nbz)
    live = planes[LIVE] > 0.5
    new_planes[LIVE] = planes[LIVE]
    state = advance(sampled, live, frac, vel, stress)
    store_state(state, new_frac, new_vel, new_stress)
    m = jnp.where(live, mass[...], 0.0)
    s = jnp.where(live, state[2], 0.0)
    prepare(cell[...], state[0], new_planes, (m, state[1], s))
    deposit(new_planes, left, right_w, outer, OUTER, nby, nbz)
    side.send(outer, new_first, new_second)


def inner_pass_kernel(nby, nbz, planes, sampled, inner, left, right_w, right_d, spread, nodes):
    clear(right_w)
    clear(right_d)
    deposit(planes, left, right_w, inner, INNER, nby, nbz)
    _, vel = node_velocity(inner)
    for k in range(3):
        nodes[k] = vel[k]
    gather(planes, nodes, spread, sampled, right_w, right_d, INNER, nby, nbz)


def last_kernel(nby, nbz, frac, vel, stress, planes, partial, outer, first, second,
                new_frac, new_vel, new_stress, right_w, right_d, spread, sampled, nodes):
    side = Side()
    clear(right_w)
    clear(right_d)
    low, high = side.layers(outer, first, second)
    _, node_vel = node_velocity(jnp.concatenate([low, high], axis=1))
    for k in range(3):
        nodes[k] = side.keep(node_vel[k])
    gather(planes, nodes, spread, sampled, right_w, right_d, OUTER, nby, nbz)
    sampled[...] += partial[...]
    store_state(advance(sampled, planes[LIVE] > 0.5, frac, vel, stress), new_frac, new_vel, new_stress)


def call(kernel, name, outs, scratch, *args, space=pltpu.VMEM, cost=None, limit=24 << 20):
    spec = pl.BlockSpec(memory_space=space)
    vmem = pl.BlockSpec(memory_space=pltpu.VMEM)
    return pl.pallas_call(
        kernel,
        name=name,
        out_shape=[jax.ShapeDtypeStruct(s, F32) for s in outs],
        in_specs=[spec] * len(args),
        out_specs=[vmem] * len(outs),
        scratch_shapes=scratch,
        cost_estimate=cost,
        compiler_params=pltpu.CompilerParams(vmem_limit_bytes=limit),
    )(*args)


def local(particle_cell, block_count, particle_frac, particle_vel, particle_mass, particle_stress, drag_coef):
    cell, count = particle_cell[0], block_count
    frac, vel = particle_frac[0], particle_vel[0]
    mass, stress = particle_mass[0], particle_stress[0]
    _, ny, nz = drag_coef.shape
    sizes = nby, nbz = ny // 4, nz // 4
    blocks, slots = cell.shape
    lanes = nby * GROUP * slots
    places = lax.axis_size("space")

    def matching(start):
        pairs = [(i, i) for i in range(start)]
        for i in range(start, places - 1, 2):
            pairs += [(i, i + 1), (i + 1, i)]
        return pairs + [(i, i) for i in range(len(pairs), places)]

    swap = [(i, i ^ 1) for i in range(lax.axis_size("phase"))]
    particle = (blocks, slots)
    triple = (3,) + particle
    layers = lambda channels, n: (channels, n, ny, nz)
    planes_shape = (PLANES,) + particle
    left = lambda n: pltpu.VMEM((lanes // 128, 64 * n, 128), BF16)
    right = pltpu.VMEM((lanes // 128, 4 * WINDOW, 128), BF16)
    spread = lambda n: pltpu.VMEM((32 * n, lanes), F32)
    nodes = lambda n: pltpu.VMEM(layers(3, n), F32)
    sampled = pltpu.VMEM((4,) + particle, F32)
    cost = pl.CostEstimate(flops=3 << 30, bytes_accessed=1 << 20, transcendentals=0)

    def exchange(first, second):
        second = lax.ppermute(second, "space", matching(1))
        return lax.ppermute(first, "space", matching(0)), second

    inputs = (cell, count, frac, vel, mass, stress, drag_coef)
    sent = (9, ny, nz)
    planes, outer, first, second = call(
        functools.partial(first_kernel, *sizes), "first", [planes_shape, layers(4, 4), sent, sent],
        [pltpu.VMEM(a.shape, a.dtype) for a in inputs] + [left(4), right, pltpu.SemaphoreType.DMA((7,))],
        *[pltpu.with_memory_space_constraint(a, pltpu.HBM) for a in inputs], space=pltpu.HBM)
    first, second = exchange(first, second)
    inner, = call(functools.partial(inner_kernel, *sizes), "inner", [layers(4, 2)], [left(2), right],
                  planes, cost=cost)
    fields, = call(total_kernel, "total", [layers(4, 6)], [], outer, inner, first, second)
    other = lax.ppermute(fields, "phase", swap)
    sent = (8, ny, nz)
    frac, vel, stress, planes, outer, first, second = call(
        functools.partial(middle_kernel, *sizes), "middle",
        [triple, triple, particle, planes_shape, layers(4, 4), sent, sent],
        [left(4), right, right, spread(6), sampled, nodes(6)],
        cell, *inputs[2:], planes, fields, other, first, second)
    first, second = exchange(first, second)
    partial, _ = call(functools.partial(inner_pass_kernel, *sizes), "inner_pass",
                      [(4,) + particle, layers(4, 2)], [left(2), right, right, spread(2), nodes(2)],
                      planes, cost=cost)
    frac, vel, stress = call(
        functools.partial(last_kernel, *sizes), "last", [triple, triple, particle],
        [right, right, spread(4), sampled, nodes(4)],
        frac, vel, stress, planes, partial, outer, first, second)
    return frac[None], vel[None], stress[None]


def solution(mesh):
    in_specs = (
        P("phase", "space", None),
        P("phase", "space"),
        P("phase", None, "space", None),
        P("phase", None, "space", None),
        P("phase", "space", None),
        P("phase", "space", None),
        P("space", None, None),
    )
    out_specs = (
        P("phase", None, "space", None),
        P("phase", None, "space", None),
        P("phase", "space", None),
    )
    return jax.shard_map(local, mesh=mesh, in_specs=in_specs, out_specs=out_specs, check_vma=False)
```

```python
import functools

import jax
import jax.numpy as jnp
from jax import lax
from jax.experimental import pallas as pl
from jax.experimental.pallas import tpu as pltpu
from jax.sharding import PartitionSpec as P

time_step = 0.05
gravity = 1.0
bulk_modulus = 4.0
mass_floor = 0.25
slip_floor = 0.25

F32 = jnp.float32
BF16 = jnp.bfloat16

WX, YAT, WY, ZAT, WZ, DZ = 0, 6, 7, 10, 11, 14
CHANNEL = 17
PLANES = 22
XC, YC, LIVE = 0, 1, 2

GROUP = 4
WINDOW = 24
EDGE = 1
CHANNELS = 5


def spline(frac):
    r = frac - 0.5
    low, high = 0.5 - r, 0.5 + r
    w = (0.5 * low * low, 0.75 - r * r, 0.5 * high * high)
    d = ((-1.0 - r) * w[0], -r * w[1], (1.0 - r) * w[2])
    return w, d


def place(where_at, first, values):
    k = where_at - first
    out = jnp.where(k == 2.0, values[2], 0.0)
    out = jnp.where(k == 1.0, values[1], out)
    return jnp.where(k == 0.0, values[0], out)


def halves(value):
    high = value.astype(BF16)
    return high, (value - high.astype(F32)).astype(BF16)


def prepare(cell, frac, planes, kept, mass, vel, stress, nby, nbz):
    wx, _ = spline(frac[0])
    wy, _ = spline(frac[1])
    wz, dz = spline(frac[2])
    at_x = (cell >> 4).astype(F32)
    at_y = ((cell >> 2) & 3).astype(F32)
    block = lax.broadcasted_iota(jnp.int32, cell.shape, 0)
    at_y = at_y + 4.0 * sum((block >= nbz * k).astype(F32) for k in range(1, nby))
    planes[YAT] = at_y
    planes[ZAT] = (cell & 3).astype(F32)
    for t in range(3):
        planes[WY + t] = wy[t]
        planes[WZ + t] = wz[t]
        planes[DZ + t] = dz[t]
    for x in range(6):
        planes[WX + x] = place(float(x), at_x, wx)
    position = (at_x + (frac[0] - 2.0), at_y + (frac[1] - 2.0 * nby))
    kept[XC] = position[0]
    kept[YC] = position[1]
    scaled = (4.0 * time_step) * stress
    planes[CHANNEL] = mass
    planes[CHANNEL + 1] = mass * vel[0] - scaled * position[0]
    planes[CHANNEL + 2] = mass * vel[1] - scaled * position[1]
    planes[CHANNEL + 3] = mass * vel[2]
    planes[CHANNEL + 4] = scaled


def z_rows(q):
    return 4 * q // 8 * 8, (4 * q + 5) // 8 * 8 + 8


def side_by_side(ref, rows):
    return jnp.concatenate([ref[row] for row in rows], axis=1)


def block_row(h, b, nbz):
    return b // GROUP * nbz + h * GROUP + b % GROUP


def deposit(planes, tiles, factors, right, sums, out, nby, nbz):
    sums[...] = jnp.zeros_like(sums)
    blocks = nby * GROUP

    def group(h, carry):
        for b in range(blocks):
            row, q = block_row(h, b, nbz), b % GROUP
            get = lambda k: planes[k, pl.ds(row, 8, stride=0), :]
            at = lax.broadcasted_iota(jnp.int32, (8, 128), 0).astype(F32)
            wy = place(at, get(YAT) - 1.0, [get(WY + t) for t in range(3)])
            for x in range(0, 6, 2):
                high, low = halves(jnp.concatenate([get(WX + x) * wy, get(WX + x + 1) * wy], axis=0))
                tiles[row, 8 * x : 8 * x + 16] = high
                tiles[row, 48 + 8 * x : 64 + 8 * x] = low
            first, last = z_rows(q)
            steps = (last - first) // 8
            get = lambda k: jnp.concatenate([planes[k, pl.ds(row, 8, stride=0), :]] * steps, axis=0)
            at = lax.broadcasted_iota(jnp.int32, (last - first, 128), 0).astype(F32)
            start = get(ZAT) + float(4 * q - first)
            wz = place(at, start, [get(WZ + t) for t in range(3)])
            dz = place(at, start, [get(DZ + t) for t in range(3)])
            factors[row, 0, 0 : last - first] = wz
            factors[row, 1, 0 : last - first] = dz
            parts = [get(CHANNEL + c) * wz for c in range(CHANNELS)]
            parts[3] = parts[3] + get(CHANNEL + 4) * dz
            zeros = lambda n: [jnp.zeros((n, 128), F32)] if n else []
            high = [part.astype(BF16).astype(F32) for part in parts]
            low = [part - h for part, h in zip(parts, high)]
            for at, values in ((0, high), (128, low)):
                stack = []
                for value in values:
                    stack += zeros(first) + [value] + zeros(WINDOW - last)
                stack += zeros(128 - CHANNELS * WINDOW)
                right[b, at : at + 128] = jnp.concatenate(stack, axis=0).astype(BF16)
        a = side_by_side(tiles, [block_row(h, b, nbz) for b in range(blocks)])
        o = lax.dot_general(a, side_by_side(right, range(blocks)), (((1,), (1,)), ((), ())),
                            preferred_element_type=F32)
        o = o[0:48] + o[48:96]
        o = o[:, 0:128] + o[:, 128:256]
        z = lax.broadcasted_iota(jnp.int32, o.shape, 1) - (4 * GROUP * h - EDGE)
        inside = (z >= 0) & (z < WINDOW)
        for c in range(CHANNELS):
            moved = pltpu.roll(o, lax.rem(4 * GROUP * h + (128 - EDGE + 128 - WINDOW * c), 128), 1)
            sums[c] += jnp.where(inside, moved, 0.0)
        return carry

    lax.fori_loop(0, nbz // GROUP, group, 0, unroll=2)
    shape = out.shape[1:]
    x = lax.broadcasted_iota(jnp.int32, shape, 0).astype(F32) - 2.5
    y = lax.broadcasted_iota(jnp.int32, shape, 1).astype(F32) + (0.5 - 2.0 * nby)
    mass, mx, my, mz, stress = (sums[c].reshape(shape) for c in range(CHANNELS))
    out[0] = mass
    out[1] = mx + x * stress
    out[2] = my + y * stress
    out[3] = mz


def gather(vel, tiles, factors, turned, sampled, nby, nbz):
    blocks = nby * GROUP
    shape = vel[0].shape
    x = lax.broadcasted_iota(jnp.int32, shape, 0).astype(F32) - 2.5
    y = lax.broadcasted_iota(jnp.int32, shape, 1).astype(F32) + (0.5 - 2.0 * nby)
    for c, v in enumerate((vel[0], vel[1], vel[2], x * vel[0] + y * vel[1])):
        v = v.reshape(48, 128)
        high = v.astype(BF16).astype(F32)
        v = jnp.concatenate([high, v - high, jnp.zeros((32, 128), F32)], axis=0)
        turned[c, 0:8] = jnp.zeros((8, 128), F32)
        turned[c, 128:152] = jnp.zeros((24, 128), F32)
        turned[c, EDGE : EDGE + 128] = v.T
    pad = jnp.zeros((32, 128), F32).astype(BF16)

    def group(h, carry):
        at = pl.multiple_of(4 * GROUP * h, 8)
        v = jnp.concatenate([turned[c, pl.ds(at, WINDOW)] for c in range(4)], axis=0).astype(BF16)
        rows = [block_row(h, b, nbz) for b in range(blocks)]
        stack = []
        for part in (0, 48):
            piece = jnp.concatenate([tiles[row, part : part + 48] for row in rows], axis=1)
            stack += [piece, piece, jnp.concatenate([pad] * blocks, axis=1)]
        t = jnp.dot(jnp.concatenate([v, v], axis=1), jnp.concatenate(stack, axis=0), preferred_element_type=F32)
        for b, row in enumerate(rows):
            first, last = z_rows(b % GROUP)
            w, d = factors[row, 0, 0 : last - first], factors[row, 1, 0 : last - first]
            read = lambda c: t[WINDOW * c + first : WINDOW * c + last, 128 * b : 128 * b + 128]
            vz = read(2)
            for c, value in enumerate((w * read(0), w * read(1), w * vz, w * read(3) + d * vz)):
                sampled[c, pl.ds(row, 1), :] = jnp.sum(value, axis=0, keepdims=True)
        return carry

    lax.fori_loop(0, nbz // GROUP, group, 0, unroll=2)


def node_velocity(fields):
    mass = fields[0]
    inverse = 1.0 / jnp.maximum(mass, mass_floor)
    vel = [fields[k] * inverse for k in (1, 2, 3)]
    lifted = vel[2] - time_step * gravity
    floor = lax.broadcasted_iota(jnp.int32, lifted.shape, 2) == 0
    vel[2] = jnp.where(floor, jnp.maximum(lifted, 0.0), lifted)
    return mass, vel


def dragged(mass, vel, other_mass, other_vel, coef):
    slip = [b - a for a, b in zip(vel, other_vel)]
    rate = coef * jnp.sqrt(slip[0] * slip[0] + slip[1] * slip[1] + slip[2] * slip[2] + slip_floor)
    share = rate / (1.0 + rate) * (other_mass / (mass + other_mass + mass_floor))
    return [a + share * s for a, s in zip(vel, slip)]


class Side:
    def __init__(self):
        place_id = lax.axis_index("space")
        self.even = lax.rem(place_id, 2) == 0
        self.has_left = place_id > 0
        self.has_right = place_id < lax.axis_size("space") - 1

    def arrived(self, first, second, rows):
        first, second = first[rows], second[rows]
        from_left = jnp.where(self.even, second, first)
        from_right = jnp.where(self.even, first, second)
        return jnp.where(self.has_left, from_left, 0.0), jnp.where(self.has_right, from_right, 0.0)

    def layers(self, own, first, second):
        left, right = self.arrived(first, second, slice(0, 8))
        shape = (4, 2) + left.shape[1:]
        own = own[...]
        return jnp.concatenate(
            [own[:, 0:2] + left.reshape(shape), own[:, 2:4], own[:, 4:6] + right.reshape(shape)], axis=1
        )

    def send(self, own, first, second, coef=None):
        toward = jnp.where(self.even, 4, 0)
        for ref, start in ((first, toward), (second, 4 - toward)):
            for c in range(4):
                ref[2 * c : 2 * c + 2] = own[c, pl.ds(start, 2)]
        if coef is not None:
            first[8] = jnp.where(self.even, coef[3], coef[0])
            second[8] = jnp.where(self.even, coef[0], coef[3])

    def keep(self, vel):
        layer = lax.broadcasted_iota(jnp.int32, vel.shape, 0)
        keep = ((layer > 0) | self.has_left) & ((layer < vel.shape[0] - 1) | self.has_right)
        return jnp.where(keep, vel, 0.0)


def live_mask(count, shape):
    square = (shape[0], shape[0])
    same = lax.broadcasted_iota(jnp.int32, square, 0) == lax.broadcasted_iota(jnp.int32, square, 1)
    column = jnp.sum(jnp.where(same, count[...].astype(F32), 0.0), axis=1, keepdims=True)
    return lax.broadcasted_iota(jnp.int32, shape, 1).astype(F32) < column


def advance(sampled, kept, frac_ref, vel_ref, stress_ref):
    live = kept[LIVE] > 0.5
    vel = [sampled[k] for k in range(3)]
    rate = sampled[3] - kept[XC] * vel[0] - kept[YC] * vel[1]
    old = stress_ref[...]
    stress = jnp.where(live, old - (time_step * bulk_modulus * 4.0) * rate, old)
    frac = [jnp.where(live, frac_ref[k] + time_step * vel[k], frac_ref[k]) for k in range(3)]
    vel = [jnp.where(live, vel[k], vel_ref[k]) for k in range(3)]
    return frac, vel, stress


def store_state(state, new_frac, new_vel, new_stress):
    frac, vel, stress = state
    for k in range(3):
        new_frac[k] = frac[k]
        new_vel[k] = vel[k]
    new_stress[...] = stress


def first_kernel(sizes, *refs):
    sources, (kept, tiles, factors, dep, first, second), rest = refs[:7], refs[7:13], refs[13:]
    inputs, (planes, right, sums, sems) = rest[:7], rest[7:]
    copies = [pltpu.make_async_copy(a, b, sems.at[k]) for k, (a, b) in enumerate(zip(sources, inputs))]
    for copy in copies:
        copy.start()
    for copy in copies:
        copy.wait()
    cell, count, frac, vel, mass, stress, coef = inputs
    live = live_mask(count, cell.shape)
    kept[LIVE] = jnp.where(live, 1.0, 0.0)
    m = jnp.where(live, mass[...], 0.0)
    s = jnp.where(live, stress[...], 0.0)
    prepare(cell[...], [frac[k] for k in range(3)], planes, kept, m, [vel[k] for k in range(3)], s, *sizes)
    deposit(planes, tiles, factors, right, sums, dep, *sizes)
    Side().send(dep, first, second, coef)


def total_kernel(dep, first, second, fields):
    fields[...] = Side().layers(dep, first, second)


def middle_kernel(sizes, cell, frac, vel, mass, stress, coef, kept, tiles, factors, fields, other, first, second,
                  new_frac, new_vel, new_stress, new_kept, new_tiles, new_factors, dep, new_first, new_second,
                  planes, right, sums, turned, sampled):
    side = Side()
    own_mass, own_vel = node_velocity(fields)
    other_mass, other_vel = node_velocity(other)
    low, high = side.arrived(first, second, slice(8, 9))
    coefs = jnp.concatenate([low, coef[...], high], axis=0)
    nodes = [side.keep(v) for v in dragged(own_mass, own_vel, other_mass, other_vel, coefs)]
    gather(nodes, tiles, factors, turned, sampled, *sizes)
    state = advance(sampled, kept, frac, vel, stress)
    store_state(state, new_frac, new_vel, new_stress)
    new_kept[LIVE] = kept[LIVE]
    live = kept[LIVE] > 0.5
    m = jnp.where(live, mass[...], 0.0)
    s = jnp.where(live, state[2], 0.0)
    prepare(cell[...], state[0], planes, new_kept, m, state[1], s, *sizes)
    deposit(planes, new_tiles, new_factors, right, sums, dep, *sizes)
    side.send(dep, new_first, new_second)


def last_kernel(sizes, frac, vel, stress, kept, tiles, factors, dep, first, second,
                new_frac, new_vel, new_stress, turned, sampled):
    side = Side()
    _, nodes = node_velocity(side.layers(dep, first, second))
    gather([side.keep(v) for v in nodes], tiles, factors, turned, sampled, *sizes)
    store_state(advance(sampled, kept, frac, vel, stress), new_frac, new_vel, new_stress)


def call(kernel, name, outs, scratch, *args, space=pltpu.VMEM, cost=None, limit=24 << 20):
    spec = pl.BlockSpec(memory_space=space)
    vmem = pl.BlockSpec(memory_space=pltpu.VMEM)
    return pl.pallas_call(
        kernel,
        name=name,
        out_shape=[jax.ShapeDtypeStruct(*(s if isinstance(s[0], tuple) else (s, F32))) for s in outs],
        in_specs=[spec] * len(args),
        out_specs=[vmem] * len(outs),
        scratch_shapes=scratch,
        cost_estimate=cost,
        compiler_params=pltpu.CompilerParams(vmem_limit_bytes=limit),
    )(*args)


def local(particle_cell, block_count, particle_frac, particle_vel, particle_mass, particle_stress, drag_coef):
    cell, count = particle_cell[0], block_count
    frac, vel = particle_frac[0], particle_vel[0]
    mass, stress = particle_mass[0], particle_stress[0]
    layers, ny, nz = drag_coef.shape
    sizes = nby, nbz = ny // 4, nz // 4
    blocks, slots = cell.shape
    places = lax.axis_size("space")

    def matching(start):
        pairs = [(i, i) for i in range(start)]
        for i in range(start, places - 1, 2):
            pairs += [(i, i + 1), (i + 1, i)]
        return pairs + [(i, i) for i in range(len(pairs), places)]

    swap = [(i, i ^ 1) for i in range(lax.axis_size("phase"))]
    particle = (blocks, slots)
    triple = (3,) + particle
    grid = (4, layers + 2, ny, nz)
    saved = [triple, ((blocks, 96, slots), BF16), (blocks, 2, 16, slots)]
    planes = pltpu.VMEM((PLANES,) + particle, F32)
    right = pltpu.VMEM((nby * GROUP, 256, slots), BF16)
    sums = pltpu.VMEM((CHANNELS, (layers + 2) * ny, nz), F32)
    turned = pltpu.VMEM((4, nz + 24, 128), F32)
    sampled = pltpu.VMEM((4,) + particle, F32)

    def exchange(first, second):
        second = lax.ppermute(second, "space", matching(1))
        return lax.ppermute(first, "space", matching(0)), second

    inputs = (cell, count, frac, vel, mass, stress, drag_coef)
    sent = (9, ny, nz)
    kept, tiles, factors, dep, first, second = call(
        functools.partial(first_kernel, sizes), "first", saved + [grid, sent, sent],
        [pltpu.VMEM(a.shape, a.dtype) for a in inputs] + [planes, right, sums, pltpu.SemaphoreType.DMA((7,))],
        *[pltpu.with_memory_space_constraint(a, pltpu.HBM) for a in inputs], space=pltpu.HBM)
    first, second = exchange(first, second)
    fields, = call(total_kernel, "total", [grid], [], dep, first, second)
    other = lax.ppermute(fields, "phase", swap)
    sent = (8, ny, nz)
    frac, vel, stress, kept, tiles, factors, dep, first, second = call(
        functools.partial(middle_kernel, sizes), "middle",
        [triple, triple, particle] + saved + [grid, sent, sent],
        [planes, right, sums, turned, sampled],
        cell, *inputs[2:], kept, tiles, factors, fields, other, first, second)
    first, second = exchange(first, second)
    frac, vel, stress = call(
        functools.partial(last_kernel, sizes), "last", [triple, triple, particle], [turned, sampled],
        frac, vel, stress, kept, tiles, factors, dep, first, second)
    return frac[None], vel[None], stress[None]


def solution(mesh):
    in_specs = (
        P("phase", "space", None),
        P("phase", "space"),
        P("phase", None, "space", None),
        P("phase", None, "space", None),
        P("phase", "space", None),
        P("phase", "space", None),
        P("space", None, None),
    )
    out_specs = (
        P("phase", None, "space", None),
        P("phase", None, "space", None),
        P("phase", "space", None),
    )
    return jax.shard_map(local, mesh=mesh, in_specs=in_specs, out_specs=out_specs, check_vma=False)
```

```python
import functools

import jax
import jax.numpy as jnp
from jax import lax
from jax.experimental import pallas as pl
from jax.experimental.pallas import tpu as pltpu
from jax.sharding import PartitionSpec as P

time_step = 0.05
gravity = 1.0
bulk_modulus = 4.0
mass_floor = 0.25
slip_floor = 0.25

F32 = jnp.float32
BF16 = jnp.bfloat16

WX, YAT, WY, ZAT, WZ, DZ = 0, 6, 7, 10, 11, 14
CHANNEL = 17
PLANES = 22
XC, YC, LIVE = 0, 1, 2

GROUP = 4
WINDOW = 24
EDGE = 1
CHANNELS = 5


def spline(frac):
    r = frac - 0.5
    low, high = 0.5 - r, 0.5 + r
    w = (0.5 * low * low, 0.75 - r * r, 0.5 * high * high)
    d = ((-1.0 - r) * w[0], -r * w[1], (1.0 - r) * w[2])
    return w, d


def place(where_at, first, values):
    k = where_at - first
    out = jnp.where(k == 2.0, values[2], 0.0)
    out = jnp.where(k == 1.0, values[1], out)
    return jnp.where(k == 0.0, values[0], out)


def halves(value):
    high = value.astype(BF16)
    return high, (value - high.astype(F32)).astype(BF16)


def prepare(cell, frac, planes, kept, mass, vel, stress, nby, nbz):
    wx, _ = spline(frac[0])
    wy, _ = spline(frac[1])
    wz, dz = spline(frac[2])
    at_x = (cell >> 4).astype(F32)
    at_y = ((cell >> 2) & 3).astype(F32)
    block = lax.broadcasted_iota(jnp.int32, cell.shape, 0)
    at_y = at_y + 4.0 * sum((block >= nbz * k).astype(F32) for k in range(1, nby))
    planes[YAT] = at_y
    planes[ZAT] = (cell & 3).astype(F32)
    for t in range(3):
        planes[WY + t] = wy[t]
        planes[WZ + t] = wz[t]
        planes[DZ + t] = dz[t]
    for x in range(6):
        planes[WX + x] = place(float(x), at_x, wx)
    position = (at_x + (frac[0] - 2.0), at_y + (frac[1] - 2.0 * nby))
    kept[XC] = position[0]
    kept[YC] = position[1]
    scaled = (4.0 * time_step) * stress
    planes[CHANNEL] = mass
    planes[CHANNEL + 1] = mass * vel[0] - scaled * position[0]
    planes[CHANNEL + 2] = mass * vel[1] - scaled * position[1]
    planes[CHANNEL + 3] = mass * vel[2]
    planes[CHANNEL + 4] = scaled


def z_rows(q):
    return 4 * q // 8 * 8, (4 * q + 5) // 8 * 8 + 8


def side_by_side(ref, rows):
    return jnp.concatenate([ref[row] for row in rows], axis=1)


def block_row(h, b, nbz):
    return b // GROUP * nbz + h * GROUP + b % GROUP


def deposit(planes, tiles, factors, right, sums, out, nby, nbz):
    sums[...] = jnp.zeros_like(sums)
    blocks = nby * GROUP

    def group(h, carry):
        for b in range(blocks):
            row, q = block_row(h, b, nbz), b % GROUP
            get = lambda k: planes[k, pl.ds(row, 8, stride=0), :]
            at = lax.broadcasted_iota(jnp.int32, (8, 128), 0).astype(F32)
            wy = place(at, get(YAT) - 1.0, [get(WY + t) for t in range(3)])
            for x in range(0, 6, 2):
                high, low = halves(jnp.concatenate([get(WX + x) * wy, get(WX + x + 1) * wy], axis=0))
                tiles[row, 8 * x : 8 * x + 16] = high
                tiles[row, 48 + 8 * x : 64 + 8 * x] = low
            first, last = z_rows(q)
            steps = (last - first) // 8
            get = lambda k: jnp.concatenate([planes[k, pl.ds(row, 8, stride=0), :]] * steps, axis=0)
            at = lax.broadcasted_iota(jnp.int32, (last - first, 128), 0).astype(F32)
            start = get(ZAT) + float(4 * q - first)
            wz = place(at, start, [get(WZ + t) for t in range(3)])
            dz = place(at, start, [get(DZ + t) for t in range(3)])
            factors[row, 0, 0 : last - first] = wz
            factors[row, 1, 0 : last - first] = dz
            parts = [get(CHANNEL + c) * wz for c in range(CHANNELS)]
            parts[3] = parts[3] + get(CHANNEL + 4) * dz
            zeros = lambda n: [jnp.zeros((n, 128), F32)] if n else []
            high = [part.astype(BF16).astype(F32) for part in parts]
            low = [part - h for part, h in zip(parts, high)]
            for at, values in ((0, high), (128, low)):
                stack = []
                for value in values:
                    stack += zeros(first) + [value] + zeros(WINDOW - last)
                stack += zeros(128 - CHANNELS * WINDOW)
                right[b, at : at + 128] = jnp.concatenate(stack, axis=0).astype(BF16)
        a = side_by_side(tiles, [block_row(h, b, nbz) for b in range(blocks)])
        o = lax.dot_general(a, side_by_side(right, range(blocks)), (((1,), (1,)), ((), ())),
                            preferred_element_type=F32)
        o = o[0:48] + o[48:96]
        o = o[:, 0:128] + o[:, 128:256]
        z = lax.broadcasted_iota(jnp.int32, o.shape, 1) - (4 * GROUP * h - EDGE)
        inside = (z >= 0) & (z < WINDOW)
        for c in range(CHANNELS):
            moved = pltpu.roll(o, lax.rem(4 * GROUP * h + (128 - EDGE + 128 - WINDOW * c), 128), 1)
            sums[c] += jnp.where(inside, moved, 0.0)
        return carry

    lax.fori_loop(0, nbz // GROUP, group, 0, unroll=True)
    shape = out.shape[1:]
    x = lax.broadcasted_iota(jnp.int32, shape, 0).astype(F32) - 2.5
    y = lax.broadcasted_iota(jnp.int32, shape, 1).astype(F32) + (0.5 - 2.0 * nby)
    mass, mx, my, mz, stress = (sums[c].reshape(shape) for c in range(CHANNELS))
    out[0] = mass
    out[1] = mx + x * stress
    out[2] = my + y * stress
    out[3] = mz


def gather(vel, tiles, factors, turned, sampled, nby, nbz):
    blocks = nby * GROUP
    shape = vel[0].shape
    x = lax.broadcasted_iota(jnp.int32, shape, 0).astype(F32) - 2.5
    y = lax.broadcasted_iota(jnp.int32, shape, 1).astype(F32) + (0.5 - 2.0 * nby)
    for c, v in enumerate((vel[0], vel[1], vel[2], x * vel[0] + y * vel[1])):
        v = v.reshape(48, 128)
        high = v.astype(BF16).astype(F32)
        v = jnp.concatenate([high, v - high, jnp.zeros((32, 128), F32)], axis=0)
        turned[c, 0:8] = jnp.zeros((8, 128), F32)
        turned[c, 128:152] = jnp.zeros((24, 128), F32)
        turned[c, EDGE : EDGE + 128] = v.T
    pad = jnp.zeros((32, 128), F32).astype(BF16)

    def group(h, carry):
        at = pl.multiple_of(4 * GROUP * h, 8)
        v = jnp.concatenate([turned[c, pl.ds(at, WINDOW)] for c in range(4)], axis=0).astype(BF16)
        rows = [block_row(h, b, nbz) for b in range(blocks)]
        stack = []
        for part in (0, 48):
            piece = jnp.concatenate([tiles[row, part : part + 48] for row in rows], axis=1)
            stack += [piece, piece, jnp.concatenate([pad] * blocks, axis=1)]
        t = jnp.dot(jnp.concatenate([v, v], axis=1), jnp.concatenate(stack, axis=0), preferred_element_type=F32)
        for b, row in enumerate(rows):
            first, last = z_rows(b % GROUP)
            w, d = factors[row, 0, 0 : last - first], factors[row, 1, 0 : last - first]
            read = lambda c: t[WINDOW * c + first : WINDOW * c + last, 128 * b : 128 * b + 128]
            vz = read(2)
            for c, value in enumerate((w * read(0), w * read(1), w * vz, w * read(3) + d * vz)):
                sampled[c, pl.ds(row, 1), :] = jnp.sum(value, axis=0, keepdims=True)
        return carry

    lax.fori_loop(0, nbz // GROUP, group, 0, unroll=True)


def node_velocity(fields):
    mass = fields[0]
    inverse = 1.0 / jnp.maximum(mass, mass_floor)
    vel = [fields[k] * inverse for k in (1, 2, 3)]
    lifted = vel[2] - time_step * gravity
    floor = lax.broadcasted_iota(jnp.int32, lifted.shape, 2) == 0
    vel[2] = jnp.where(floor, jnp.maximum(lifted, 0.0), lifted)
    return mass, vel


def dragged(mass, vel, other_mass, other_vel, coef):
    slip = [b - a for a, b in zip(vel, other_vel)]
    rate = coef * jnp.sqrt(slip[0] * slip[0] + slip[1] * slip[1] + slip[2] * slip[2] + slip_floor)
    share = rate / (1.0 + rate) * (other_mass / (mass + other_mass + mass_floor))
    return [a + share * s for a, s in zip(vel, slip)]


class Side:
    def __init__(self):
        place_id = lax.axis_index("space")
        self.even = lax.rem(place_id, 2) == 0
        self.has_left = place_id > 0
        self.has_right = place_id < lax.axis_size("space") - 1

    def arrived(self, first, second, rows):
        first, second = first[rows], second[rows]
        from_left = jnp.where(self.even, second, first)
        from_right = jnp.where(self.even, first, second)
        return jnp.where(self.has_left, from_left, 0.0), jnp.where(self.has_right, from_right, 0.0)

    def layers(self, own, first, second):
        left, right = self.arrived(first, second, slice(0, 8))
        shape = (4, 2) + left.shape[1:]
        own = own[...]
        return jnp.concatenate(
            [own[:, 0:2] + left.reshape(shape), own[:, 2:4], own[:, 4:6] + right.reshape(shape)], axis=1
        )

    def send(self, own, first, second, coef=None):
        toward = jnp.where(self.even, 4, 0)
        for ref, start in ((first, toward), (second, 4 - toward)):
            for c in range(4):
                ref[2 * c : 2 * c + 2] = own[c, pl.ds(start, 2)]
        if coef is not None:
            first[8] = jnp.where(self.even, coef[3], coef[0])
            second[8] = jnp.where(self.even, coef[0], coef[3])

    def keep(self, vel):
        layer = lax.broadcasted_iota(jnp.int32, vel.shape, 0)
        keep = ((layer > 0) | self.has_left) & ((layer < vel.shape[0] - 1) | self.has_right)
        return jnp.where(keep, vel, 0.0)


def live_mask(count, shape):
    square = (shape[0], shape[0])
    same = lax.broadcasted_iota(jnp.int32, square, 0) == lax.broadcasted_iota(jnp.int32, square, 1)
    column = jnp.sum(jnp.where(same, count[...].astype(F32), 0.0), axis=1, keepdims=True)
    return lax.broadcasted_iota(jnp.int32, shape, 1).astype(F32) < column


def advance(sampled, kept, frac_ref, vel_ref, stress_ref):
    live = kept[LIVE] > 0.5
    vel = [sampled[k] for k in range(3)]
    rate = sampled[3] - kept[XC] * vel[0] - kept[YC] * vel[1]
    old = stress_ref[...]
    stress = jnp.where(live, old - (time_step * bulk_modulus * 4.0) * rate, old)
    frac = [jnp.where(live, frac_ref[k] + time_step * vel[k], frac_ref[k]) for k in range(3)]
    vel = [jnp.where(live, vel[k], vel_ref[k]) for k in range(3)]
    return frac, vel, stress


def store_state(state, new_frac, new_vel, new_stress):
    frac, vel, stress = state
    for k in range(3):
        new_frac[k] = frac[k]
        new_vel[k] = vel[k]
    new_stress[...] = stress


def first_kernel(sizes, *refs):
    sources, inputs, rest = refs[:7], refs[7:14], refs[14:]
    kept, tiles, factors, dep, first, second, planes, right, sums, sems = rest
    copies = [pltpu.make_async_copy(a, b, sems.at[k]) for k, (a, b) in enumerate(zip(sources, inputs))]
    for copy in copies:
        copy.start()
    for copy in copies:
        copy.wait()
    cell, count, frac, vel, mass, stress, coef = inputs
    live = live_mask(count, cell.shape)
    kept[LIVE] = jnp.where(live, 1.0, 0.0)
    m = jnp.where(live, mass[...], 0.0)
    s = jnp.where(live, stress[...], 0.0)
    prepare(cell[...], [frac[k] for k in range(3)], planes, kept, m, [vel[k] for k in range(3)], s, *sizes)
    deposit(planes, tiles, factors, right, sums, dep, *sizes)
    Side().send(dep, first, second, coef)


def total_kernel(dep, first, second, fields):
    fields[...] = Side().layers(dep, first, second)


def middle_kernel(sizes, cell, frac, vel, mass, stress, coef, kept, tiles, factors, fields, other, first, second,
                  new_frac, new_vel, new_stress, new_kept, new_tiles, new_factors, dep, new_first, new_second,
                  planes, right, sums, turned, sampled):
    side = Side()
    own_mass, own_vel = node_velocity(fields)
    other_mass, other_vel = node_velocity(other)
    low, high = side.arrived(first, second, slice(8, 9))
    coefs = jnp.concatenate([low, coef[...], high], axis=0)
    nodes = [side.keep(v) for v in dragged(own_mass, own_vel, other_mass, other_vel, coefs)]
    gather(nodes, tiles, factors, turned, sampled, *sizes)
    state = advance(sampled, kept, frac, vel, stress)
    store_state(state, new_frac, new_vel, new_stress)
    new_kept[LIVE] = kept[LIVE]
    live = kept[LIVE] > 0.5
    m = jnp.where(live, mass[...], 0.0)
    s = jnp.where(live, state[2], 0.0)
    prepare(cell[...], state[0], planes, new_kept, m, state[1], s, *sizes)
    deposit(planes, new_tiles, new_factors, right, sums, dep, *sizes)
    side.send(dep, new_first, new_second)


def last_kernel(sizes, frac, vel, stress, kept, tiles, factors, dep, first, second,
                new_frac, new_vel, new_stress, turned, sampled):
    side = Side()
    _, nodes = node_velocity(side.layers(dep, first, second))
    gather([side.keep(v) for v in nodes], tiles, factors, turned, sampled, *sizes)
    store_state(advance(sampled, kept, frac, vel, stress), new_frac, new_vel, new_stress)


def call(kernel, name, outs, scratch, *args, space=pltpu.VMEM, cost=None, limit=24 << 20):
    spec = pl.BlockSpec(memory_space=space)
    vmem = pl.BlockSpec(memory_space=pltpu.VMEM)
    return pl.pallas_call(
        kernel,
        name=name,
        out_shape=[jax.ShapeDtypeStruct(*(s if isinstance(s[0], tuple) else (s, F32))) for s in outs],
        in_specs=[spec] * len(args),
        out_specs=[vmem] * len(outs),
        scratch_shapes=scratch,
        cost_estimate=cost,
        compiler_params=pltpu.CompilerParams(vmem_limit_bytes=limit),
    )(*args)


def local(particle_cell, block_count, particle_frac, particle_vel, particle_mass, particle_stress, drag_coef):
    cell, count = particle_cell[0], block_count
    frac, vel = particle_frac[0], particle_vel[0]
    mass, stress = particle_mass[0], particle_stress[0]
    layers, ny, nz = drag_coef.shape
    sizes = nby, nbz = ny // 4, nz // 4
    blocks, slots = cell.shape
    places = lax.axis_size("space")

    def matching(start):
        pairs = [(i, i) for i in range(start)]
        for i in range(start, places - 1, 2):
            pairs += [(i, i + 1), (i + 1, i)]
        return pairs + [(i, i) for i in range(len(pairs), places)]

    swap = [(i, i ^ 1) for i in range(lax.axis_size("phase"))]
    particle = (blocks, slots)
    triple = (3,) + particle
    grid = (4, layers + 2, ny, nz)
    saved = [triple, ((blocks, 96, slots), BF16), (blocks, 2, 16, slots)]
    planes = pltpu.VMEM((PLANES,) + particle, F32)
    right = pltpu.VMEM((nby * GROUP, 256, slots), BF16)
    sums = pltpu.VMEM((CHANNELS, (layers + 2) * ny, nz), F32)
    turned = pltpu.VMEM((4, nz + 24, 128), F32)
    sampled = pltpu.VMEM((4,) + particle, F32)

    def exchange(first, second):
        second = lax.ppermute(second, "space", matching(1))
        return lax.ppermute(first, "space", matching(0)), second

    inputs = (cell, count, frac, vel, mass, stress, drag_coef)
    sent = (9, ny, nz)
    *loaded, kept, tiles, factors, dep, first, second = call(
        functools.partial(first_kernel, sizes), "first",
        [(a.shape, a.dtype) for a in inputs] + saved + [grid, sent, sent],
        [planes, right, sums, pltpu.SemaphoreType.DMA((7,))],
        *[pltpu.with_memory_space_constraint(a, pltpu.HBM) for a in inputs], space=pltpu.HBM)
    first, second = exchange(first, second)
    fields, = call(total_kernel, "total", [grid], [], dep, first, second)
    other = lax.ppermute(fields, "phase", swap)
    sent = (8, ny, nz)
    frac, vel, stress, kept, tiles, factors, dep, first, second = call(
        functools.partial(middle_kernel, sizes), "middle",
        [triple, triple, particle] + saved + [grid, sent, sent],
        [planes, right, sums, turned, sampled],
        loaded[0], *loaded[2:], kept, tiles, factors, fields, other, first, second)
    first, second = exchange(first, second)
    frac, vel, stress = call(
        functools.partial(last_kernel, sizes), "last", [triple, triple, particle], [turned, sampled],
        frac, vel, stress, kept, tiles, factors, dep, first, second)
    return frac[None], vel[None], stress[None]


def solution(mesh):
    in_specs = (
        P("phase", "space", None),
        P("phase", "space"),
        P("phase", None, "space", None),
        P("phase", None, "space", None),
        P("phase", "space", None),
        P("phase", "space", None),
        P("space", None, None),
    )
    out_specs = (
        P("phase", None, "space", None),
        P("phase", None, "space", None),
        P("phase", "space", None),
    )
    return jax.shard_map(local, mesh=mesh, in_specs=in_specs, out_specs=out_specs, check_vma=False)
```

```python
import functools

import jax
import jax.numpy as jnp
from jax import lax
from jax.experimental import pallas as pl
from jax.experimental.pallas import tpu as pltpu
from jax.sharding import PartitionSpec as P


time_step = 0.05
gravity = 1.0
bulk_modulus = 4.0
mass_floor = 0.25
slip_floor = 0.25

F32 = jnp.float32
BF16 = jnp.bfloat16

WX, YAT, WY, ZAT, WZ, DZ = 0, 6, 7, 10, 11, 14
CHANNEL = 17
PLANES = 22
XC, YC, LIVE = 0, 1, 2

GROUP = 4
WINDOW = 24
EDGE = 1
CHANNELS = 5


def spline(frac):
    r = frac - 0.5
    low, high = 0.5 - r, 0.5 + r
    w = (0.5 * low * low, 0.75 - r * r, 0.5 * high * high)
    d = ((-1.0 - r) * w[0], -r * w[1], (1.0 - r) * w[2])
    return w, d


def place(where_at, first, values):
    k = where_at - first
    out = jnp.where(k == 2.0, values[2], 0.0)
    out = jnp.where(k == 1.0, values[1], out)
    return jnp.where(k == 0.0, values[0], out)


def halves(value):
    high = value.astype(BF16)
    return high, (value - high.astype(F32)).astype(BF16)


def prepare(cell, frac, planes, kept, mass, vel, stress, nby, nbz):
    wx, _ = spline(frac[0])
    wy, _ = spline(frac[1])
    wz, dz = spline(frac[2])
    at_x = (cell >> 4).astype(F32)
    at_y = ((cell >> 2) & 3).astype(F32)
    block = lax.broadcasted_iota(jnp.int32, cell.shape, 0)
    at_y = at_y + 4.0 * sum((block >= nbz * k).astype(F32) for k in range(1, nby))
    planes[YAT] = at_y
    planes[ZAT] = (cell & 3).astype(F32)
    for t in range(3):
        planes[WY + t] = wy[t]
        planes[WZ + t] = wz[t]
        planes[DZ + t] = dz[t]
    for x in range(6):
        planes[WX + x] = place(float(x), at_x, wx)
    position = (at_x + (frac[0] - 2.0), at_y + (frac[1] - 2.0 * nby))
    kept[XC] = position[0]
    kept[YC] = position[1]
    scaled = (4.0 * time_step) * stress
    planes[CHANNEL] = mass
    planes[CHANNEL + 1] = mass * vel[0] - scaled * position[0]
    planes[CHANNEL + 2] = mass * vel[1] - scaled * position[1]
    planes[CHANNEL + 3] = mass * vel[2]
    planes[CHANNEL + 4] = scaled


def z_rows(q):
    return 4 * q // 8 * 8, (4 * q + 5) // 8 * 8 + 8


def side_by_side(ref, rows):
    return jnp.concatenate([ref[row] for row in rows], axis=1)


def block_row(h, b, nbz):
    return b // GROUP * nbz + h * GROUP + b % GROUP


def deposit(planes, tiles, factors, right, sums, out, nby, nbz):
    sums[...] = jnp.zeros_like(sums)
    blocks = nby * GROUP

    def group(h, carry):
        for b in range(blocks):
            row, q = block_row(h, b, nbz), b % GROUP
            get = lambda k: planes[k, pl.ds(row, 8, stride=0), :]
            at = lax.broadcasted_iota(jnp.int32, (8, 128), 0).astype(F32)
            wy = place(at, get(YAT) - 1.0, [get(WY + t) for t in range(3)])
            for x in range(0, 6, 2):
                high, low = halves(jnp.concatenate([get(WX + x) * wy, get(WX + x + 1) * wy], axis=0))
                tiles[row, 8 * x : 8 * x + 16] = high
                tiles[row, 48 + 8 * x : 64 + 8 * x] = low
            first, last = z_rows(q)
            steps = (last - first) // 8
            get = lambda k: jnp.concatenate([planes[k, pl.ds(row, 8, stride=0), :]] * steps, axis=0)
            at = lax.broadcasted_iota(jnp.int32, (last - first, 128), 0).astype(F32)
            start = get(ZAT) + float(4 * q - first)
            wz = place(at, start, [get(WZ + t) for t in range(3)])
            dz = place(at, start, [get(DZ + t) for t in range(3)])
            factors[row, 0, 0 : last - first] = wz
            factors[row, 1, 0 : last - first] = dz
            parts = [get(CHANNEL + c) * wz for c in range(CHANNELS)]
            parts[3] = parts[3] + get(CHANNEL + 4) * dz
            zeros = lambda n: [jnp.zeros((n, 128), F32)] if n else []
            high = [part.astype(BF16).astype(F32) for part in parts]
            low = [part - h for part, h in zip(parts, high)]
            for at, values in ((0, high), (128, low)):
                stack = []
                for value in values:
                    stack += zeros(first) + [value] + zeros(WINDOW - last)
                stack += zeros(128 - CHANNELS * WINDOW)
                right[b, at : at + 128] = jnp.concatenate(stack, axis=0).astype(BF16)
        a = side_by_side(tiles, [block_row(h, b, nbz) for b in range(blocks)])
        o = lax.dot_general(a, side_by_side(right, range(blocks)), (((1,), (1,)), ((), ())),
                            preferred_element_type=F32)
        o = o[0:48] + o[48:96]
        o = o[:, 0:128] + o[:, 128:256]
        z = lax.broadcasted_iota(jnp.int32, o.shape, 1) - (4 * GROUP * h - EDGE)
        inside = (z >= 0) & (z < WINDOW)
        for c in range(CHANNELS):
            moved = pltpu.roll(o, lax.rem(4 * GROUP * h + (128 - EDGE + 128 - WINDOW * c), 128), 1)
            sums[c] += jnp.where(inside, moved, 0.0)
        return carry

    lax.fori_loop(0, nbz // GROUP, group, 0, unroll=True)
    shape = out.shape[1:]
    x = lax.broadcasted_iota(jnp.int32, shape, 0).astype(F32) - 2.5
    y = lax.broadcasted_iota(jnp.int32, shape, 1).astype(F32) + (0.5 - 2.0 * nby)
    mass, mx, my, mz, stress = (sums[c].reshape(shape) for c in range(CHANNELS))
    out[0] = mass
    out[1] = mx + x * stress
    out[2] = my + y * stress
    out[3] = mz


def gather(vel, tiles, factors, turned, sampled, nby, nbz):
    blocks = nby * GROUP
    shape = vel[0].shape
    x = lax.broadcasted_iota(jnp.int32, shape, 0).astype(F32) - 2.5
    y = lax.broadcasted_iota(jnp.int32, shape, 1).astype(F32) + (0.5 - 2.0 * nby)
    for c, v in enumerate((vel[0], vel[1], vel[2], x * vel[0] + y * vel[1])):
        v = v.reshape(48, 128)
        high = v.astype(BF16).astype(F32)
        v = jnp.concatenate([high, v - high, jnp.zeros((32, 128), F32)], axis=0)
        turned[c, 0:8] = jnp.zeros((8, 128), F32)
        turned[c, 128:152] = jnp.zeros((24, 128), F32)
        turned[c, EDGE : EDGE + 128] = v.T
    pad = jnp.zeros((32, 128), F32).astype(BF16)

    def group(h, carry):
        at = pl.multiple_of(4 * GROUP * h, 8)
        v = jnp.concatenate([turned[c, pl.ds(at, WINDOW)] for c in range(4)], axis=0).astype(BF16)
        rows = [block_row(h, b, nbz) for b in range(blocks)]
        stack = []
        for part in (0, 48):
            piece = jnp.concatenate([tiles[row, part : part + 48] for row in rows], axis=1)
            stack += [piece, piece, jnp.concatenate([pad] * blocks, axis=1)]
        t = jnp.dot(jnp.concatenate([v, v], axis=1), jnp.concatenate(stack, axis=0), preferred_element_type=F32)
        for b, row in enumerate(rows):
            first, last = z_rows(b % GROUP)
            w, d = factors[row, 0, 0 : last - first], factors[row, 1, 0 : last - first]
            read = lambda c: t[WINDOW * c + first : WINDOW * c + last, 128 * b : 128 * b + 128]
            vz = read(2)
            for c, value in enumerate((w * read(0), w * read(1), w * vz, w * read(3) + d * vz)):
                sampled[c, pl.ds(row, 1), :] = jnp.sum(value, axis=0, keepdims=True)
        return carry

    lax.fori_loop(0, nbz // GROUP, group, 0, unroll=True)


def node_velocity(fields):
    mass = fields[0]
    inverse = 1.0 / jnp.maximum(mass, mass_floor)
    vel = [fields[k] * inverse for k in (1, 2, 3)]
    lifted = vel[2] - time_step * gravity
    floor = lax.broadcasted_iota(jnp.int32, lifted.shape, 2) == 0
    vel[2] = jnp.where(floor, jnp.maximum(lifted, 0.0), lifted)
    return mass, vel


def dragged(mass, vel, other_mass, other_vel, coef):
    slip = [b - a for a, b in zip(vel, other_vel)]
    rate = coef * jnp.sqrt(slip[0] * slip[0] + slip[1] * slip[1] + slip[2] * slip[2] + slip_floor)
    share = rate / (1.0 + rate) * (other_mass / (mass + other_mass + mass_floor))
    return [a + share * s for a, s in zip(vel, slip)]


class Side:
    def __init__(self):
        place_id = lax.axis_index("space")
        self.even = lax.rem(place_id, 2) == 0
        self.has_left = place_id > 0
        self.has_right = place_id < lax.axis_size("space") - 1

    def arrived(self, first, second, rows):
        first, second = first[rows], second[rows]
        from_left = jnp.where(self.even, second, first)
        from_right = jnp.where(self.even, first, second)
        return jnp.where(self.has_left, from_left, 0.0), jnp.where(self.has_right, from_right, 0.0)

    def layers(self, own, first, second):
        left, right = self.arrived(first, second, slice(0, 8))
        shape = (4, 2) + left.shape[1:]
        own = own[...]
        return jnp.concatenate(
            [own[:, 0:2] + left.reshape(shape), own[:, 2:4], own[:, 4:6] + right.reshape(shape)], axis=1
        )

    def send(self, own, first, second, coef=None):
        toward = jnp.where(self.even, 4, 0)
        for ref, start in ((first, toward), (second, 4 - toward)):
            for c in range(4):
                ref[2 * c : 2 * c + 2] = own[c, pl.ds(start, 2)]
        if coef is not None:
            first[8] = jnp.where(self.even, coef[3], coef[0])
            second[8] = jnp.where(self.even, coef[0], coef[3])

    def keep(self, vel):
        layer = lax.broadcasted_iota(jnp.int32, vel.shape, 0)
        keep = ((layer > 0) | self.has_left) & ((layer < vel.shape[0] - 1) | self.has_right)
        return jnp.where(keep, vel, 0.0)


def live_mask(count, shape):
    square = (shape[0], shape[0])
    same = lax.broadcasted_iota(jnp.int32, square, 0) == lax.broadcasted_iota(jnp.int32, square, 1)
    column = jnp.sum(jnp.where(same, count[...].astype(F32), 0.0), axis=1, keepdims=True)
    return lax.broadcasted_iota(jnp.int32, shape, 1).astype(F32) < column


def advance(sampled, kept, frac_ref, vel_ref, stress_ref):
    live = kept[LIVE] > 0.5
    vel = [sampled[k] for k in range(3)]
    rate = sampled[3] - kept[XC] * vel[0] - kept[YC] * vel[1]
    old = stress_ref[...]
    stress = jnp.where(live, old - (time_step * bulk_modulus * 4.0) * rate, old)
    frac = [jnp.where(live, frac_ref[k] + time_step * vel[k], frac_ref[k]) for k in range(3)]
    vel = [jnp.where(live, vel[k], vel_ref[k]) for k in range(3)]
    return frac, vel, stress


def store_state(state, new_frac, new_vel, new_stress):
    frac, vel, stress = state
    for k in range(3):
        new_frac[k] = frac[k]
        new_vel[k] = vel[k]
    new_stress[...] = stress


def first_kernel(sizes, *refs):
    sources, inputs, rest = refs[:7], refs[7:14], refs[14:]
    kept, tiles, factors, dep, first, second, planes, right, sums, sems = rest
    copies = [pltpu.make_async_copy(a, b, sems.at[k]) for k, (a, b) in enumerate(zip(sources, inputs))]
    for copy in copies:
        copy.start()
    for copy in copies:
        copy.wait()
    cell, count, frac, vel, mass, stress, coef = inputs
    live = live_mask(count, cell.shape)
    kept[LIVE] = jnp.where(live, 1.0, 0.0)
    m = jnp.where(live, mass[...], 0.0)
    s = jnp.where(live, stress[...], 0.0)
    prepare(cell[...], [frac[k] for k in range(3)], planes, kept, m, [vel[k] for k in range(3)], s, *sizes)
    deposit(planes, tiles, factors, right, sums, dep, *sizes)
    Side().send(dep, first, second, coef)


def total_kernel(dep, first, second, fields):
    fields[...] = Side().layers(dep, first, second)


def middle_kernel(sizes, cell, frac, vel, mass, stress, coef, kept, tiles, factors, fields, other, first, second,
                  new_frac, new_vel, new_stress, new_kept, new_tiles, new_factors, dep, new_first, new_second,
                  planes, right, sums, turned, sampled):
    side = Side()
    own_mass, own_vel = node_velocity(fields)
    other_mass, other_vel = node_velocity(other)
    low, high = side.arrived(first, second, slice(8, 9))
    coefs = jnp.concatenate([low, coef[...], high], axis=0)
    nodes = [side.keep(v) for v in dragged(own_mass, own_vel, other_mass, other_vel, coefs)]
    gather(nodes, tiles, factors, turned, sampled, *sizes)
    state = advance(sampled, kept, frac, vel, stress)
    store_state(state, new_frac, new_vel, new_stress)
    new_kept[LIVE] = kept[LIVE]
    live = kept[LIVE] > 0.5
    m = jnp.where(live, mass[...], 0.0)
    s = jnp.where(live, state[2], 0.0)
    prepare(cell[...], state[0], planes, new_kept, m, state[1], s, *sizes)
    deposit(planes, new_tiles, new_factors, right, sums, dep, *sizes)
    side.send(dep, new_first, new_second)


def last_kernel(sizes, frac, vel, stress, kept, tiles, factors, dep, first, second,
                new_frac, new_vel, new_stress, turned, sampled):
    side = Side()
    _, nodes = node_velocity(side.layers(dep, first, second))
    gather([side.keep(v) for v in nodes], tiles, factors, turned, sampled, *sizes)
    store_state(advance(sampled, kept, frac, vel, stress), new_frac, new_vel, new_stress)


def call(kernel, outs, scratch, *args, space=pltpu.VMEM, cost=None, limit=24 << 20):
    spec = pl.BlockSpec(memory_space=space)
    vmem = pl.BlockSpec(memory_space=pltpu.VMEM)
    return pl.pallas_call(
        kernel,
        out_shape=[jax.ShapeDtypeStruct(*(s if isinstance(s[0], tuple) else (s, F32))) for s in outs],
        in_specs=[spec] * len(args),
        out_specs=[vmem] * len(outs),
        scratch_shapes=scratch,
        cost_estimate=cost,
        compiler_params=pltpu.CompilerParams(vmem_limit_bytes=limit),
    )(*args)


def local(particle_cell, block_count, particle_frac, particle_vel, particle_mass, particle_stress, drag_coef):
    cell, count = particle_cell[0], block_count
    frac, vel = particle_frac[0], particle_vel[0]
    mass, stress = particle_mass[0], particle_stress[0]
    layers, ny, nz = drag_coef.shape
    sizes = nby, nbz = ny // 4, nz // 4
    blocks, slots = cell.shape
    places = lax.axis_size("space")

    def matching(start):
        pairs = [(i, i) for i in range(start)]
        for i in range(start, places - 1, 2):
            pairs += [(i, i + 1), (i + 1, i)]
        return pairs + [(i, i) for i in range(len(pairs), places)]

    swap = [(i, i ^ 1) for i in range(lax.axis_size("phase"))]
    particle = (blocks, slots)
    triple = (3,) + particle
    grid = (4, layers + 2, ny, nz)
    saved = [triple, ((blocks, 96, slots), BF16), (blocks, 2, 16, slots)]
    planes = pltpu.VMEM((PLANES,) + particle, F32)
    right = pltpu.VMEM((nby * GROUP, 256, slots), BF16)
    sums = pltpu.VMEM((CHANNELS, (layers + 2) * ny, nz), F32)
    turned = pltpu.VMEM((4, nz + 24, 128), F32)
    sampled = pltpu.VMEM((4,) + particle, F32)

    def exchange(first, second):
        second = lax.ppermute(second, "space", matching(1))
        first = lax.ppermute(first, "space", matching(0))
        return first, second

    inputs = (cell, count, frac, vel, mass, stress, drag_coef)
    sent = (9, ny, nz)
    *loaded, kept, tiles, factors, dep, first, second = call(
        functools.partial(first_kernel, sizes),
        [(a.shape, a.dtype) for a in inputs] + saved + [grid, sent, sent],
        [planes, right, sums, pltpu.SemaphoreType.DMA((7,))],
        *[pltpu.with_memory_space_constraint(a, pltpu.HBM) for a in inputs], space=pltpu.HBM)
    first, second = exchange(first, second)
    fields, = call(total_kernel, [grid], [], dep, first, second)
    other = lax.ppermute(fields, "phase", swap)
    sent = (8, ny, nz)
    frac, vel, stress, kept, tiles, factors, dep, first, second = call(
        functools.partial(middle_kernel, sizes),
        [triple, triple, particle] + saved + [grid, sent, sent],
        [planes, right, sums, turned, sampled],
        loaded[0], *loaded[2:], kept, tiles, factors, fields, other, first, second)
    first, second = exchange(first, second)
    frac, vel, stress = call(
        functools.partial(last_kernel, sizes), [triple, triple, particle], [turned, sampled],
        frac, vel, stress, kept, tiles, factors, dep, first, second)
    return frac[None], vel[None], stress[None]


def solution(mesh):
    in_specs = (
        P("phase", "space", None),
        P("phase", "space"),
        P("phase", None, "space", None),
        P("phase", None, "space", None),
        P("phase", "space", None),
        P("phase", "space", None),
        P("space", None, None),
    )
    out_specs = (
        P("phase", None, "space", None),
        P("phase", None, "space", None),
        P("phase", "space", None),
    )
    return jax.shard_map(local, mesh=mesh, in_specs=in_specs, out_specs=out_specs, check_vma=False)
```

```python
import functools

import jax
import jax.numpy as jnp
from jax import lax
from jax.experimental import pallas as pl
from jax.experimental.pallas import tpu as pltpu
from jax.sharding import PartitionSpec as P


time_step = 0.05
gravity = 1.0
bulk_modulus = 4.0
mass_floor = 0.25
slip_floor = 0.25

F32 = jnp.float32
BF16 = jnp.bfloat16

WX, YAT, WY, ZAT, WZ, DZ = 0, 6, 7, 10, 11, 14
CHANNEL = 17
PLANES = 22
XC, YC, LIVE = 0, 1, 2

GROUP = 4
WINDOW = 24
EDGE = 1
CHANNELS = 5


def spline(frac):
    r = frac - 0.5
    low, high = 0.5 - r, 0.5 + r
    w = (0.5 * low * low, 0.75 - r * r, 0.5 * high * high)
    d = ((-1.0 - r) * w[0], -r * w[1], (1.0 - r) * w[2])
    return w, d


def place(where_at, first, values):
    k = where_at - first
    out = jnp.where(k == 2.0, values[2], 0.0)
    out = jnp.where(k == 1.0, values[1], out)
    return jnp.where(k == 0.0, values[0], out)


def halves(value):
    high = value.astype(BF16)
    return high, (value - high.astype(F32)).astype(BF16)


def prepare(cell, frac, planes, kept, mass, vel, stress, nby, nbz):
    wx, _ = spline(frac[0])
    wy, _ = spline(frac[1])
    wz, dz = spline(frac[2])
    at_x = (cell >> 4).astype(F32)
    at_y = ((cell >> 2) & 3).astype(F32)
    block = lax.broadcasted_iota(jnp.int32, cell.shape, 0)
    at_y = at_y + 4.0 * sum((block >= nbz * k).astype(F32) for k in range(1, nby))
    planes[YAT] = at_y
    planes[ZAT] = (cell & 3).astype(F32)
    for t in range(3):
        planes[WY + t] = wy[t]
        planes[WZ + t] = wz[t]
        planes[DZ + t] = dz[t]
    for x in range(6):
        planes[WX + x] = place(float(x), at_x, wx)
    position = (at_x + (frac[0] - 2.0), at_y + (frac[1] - 2.0 * nby))
    kept[XC] = position[0]
    kept[YC] = position[1]
    scaled = (4.0 * time_step) * stress
    planes[CHANNEL] = mass
    planes[CHANNEL + 1] = mass * vel[0] - scaled * position[0]
    planes[CHANNEL + 2] = mass * vel[1] - scaled * position[1]
    planes[CHANNEL + 3] = mass * vel[2]
    planes[CHANNEL + 4] = scaled


def z_rows(q):
    return 4 * q // 8 * 8, (4 * q + 5) // 8 * 8 + 8


def block_row(h, b, nbz):
    return b // GROUP * nbz + h * GROUP + b % GROUP


def deposit(planes, tiles, factors, sums, out, nby, nbz):
    sums[...] = jnp.zeros_like(sums)
    blocks = nby * GROUP

    def group(h, carry):
        columns, lines = [], []
        for b in range(blocks):
            row, q = block_row(h, b, nbz), b % GROUP
            get = lambda k: planes[k, pl.ds(row, 8, stride=0), :]
            at = lax.broadcasted_iota(jnp.int32, (8, 128), 0).astype(F32)
            wy = place(at, get(YAT) - 1.0, [get(WY + t) for t in range(3)])
            pieces = []
            for x in range(0, 6, 2):
                high, low = halves(jnp.concatenate([get(WX + x) * wy, get(WX + x + 1) * wy], axis=0))
                tiles[row, 8 * x : 8 * x + 16] = high
                tiles[row, 48 + 8 * x : 64 + 8 * x] = low
                pieces.append((high, low))
            lines.append(jnp.concatenate([p[0] for p in pieces] + [p[1] for p in pieces], axis=0))
            first, last = z_rows(q)
            steps = (last - first) // 8
            get = lambda k: jnp.concatenate([planes[k, pl.ds(row, 8, stride=0), :]] * steps, axis=0)
            at = lax.broadcasted_iota(jnp.int32, (last - first, 128), 0).astype(F32)
            start = get(ZAT) + float(4 * q - first)
            wz = place(at, start, [get(WZ + t) for t in range(3)])
            dz = place(at, start, [get(DZ + t) for t in range(3)])
            factors[row, 0, 0 : last - first] = wz
            factors[row, 1, 0 : last - first] = dz
            parts = [get(CHANNEL + c) * wz for c in range(CHANNELS)]
            parts[3] = parts[3] + get(CHANNEL + 4) * dz
            zeros = lambda n: [jnp.zeros((n, 128), F32)] if n else []
            high = [part.astype(BF16).astype(F32) for part in parts]
            low = [part - h for part, h in zip(parts, high)]
            stack = []
            for values in (high, low):
                for value in values:
                    stack += zeros(first) + [value] + zeros(WINDOW - last)
                stack += zeros(128 - CHANNELS * WINDOW)
            columns.append(jnp.concatenate(stack, axis=0).astype(BF16))
        a = jnp.concatenate(lines, axis=1)
        o = lax.dot_general(a, jnp.concatenate(columns, axis=1), (((1,), (1,)), ((), ())),
                            preferred_element_type=F32)
        o = o[0:48] + o[48:96]
        o = o[:, 0:128] + o[:, 128:256]
        z = lax.broadcasted_iota(jnp.int32, o.shape, 1) - (4 * GROUP * h - EDGE)
        inside = (z >= 0) & (z < WINDOW)
        for c in range(CHANNELS):
            moved = pltpu.roll(o, lax.rem(4 * GROUP * h + (128 - EDGE + 128 - WINDOW * c), 128), 1)
            sums[c] += jnp.where(inside, moved, 0.0)
        return carry

    lax.fori_loop(0, nbz // GROUP, group, 0, unroll=True)
    shape = out.shape[1:]
    x = lax.broadcasted_iota(jnp.int32, shape, 0).astype(F32) - 2.5
    y = lax.broadcasted_iota(jnp.int32, shape, 1).astype(F32) + (0.5 - 2.0 * nby)
    mass, mx, my, mz, stress = (sums[c].reshape(shape) for c in range(CHANNELS))
    out[0] = mass
    out[1] = mx + x * stress
    out[2] = my + y * stress
    out[3] = mz


def gather(vel, tiles, factors, turned, sampled, nby, nbz):
    blocks = nby * GROUP
    shape = vel[0].shape
    x = lax.broadcasted_iota(jnp.int32, shape, 0).astype(F32) - 2.5
    y = lax.broadcasted_iota(jnp.int32, shape, 1).astype(F32) + (0.5 - 2.0 * nby)
    for c, v in enumerate((vel[0], vel[1], vel[2], x * vel[0] + y * vel[1])):
        v = v.reshape(48, 128)
        high = v.astype(BF16).astype(F32)
        v = jnp.concatenate([high, v - high, jnp.zeros((32, 128), F32)], axis=0)
        turned[c, 0:8] = jnp.zeros((8, 128), F32)
        turned[c, 128:152] = jnp.zeros((24, 128), F32)
        turned[c, EDGE : EDGE + 128] = v.T
    pad = jnp.zeros((32, 128), F32).astype(BF16)

    def group(h, carry):
        at = pl.multiple_of(4 * GROUP * h, 8)
        v = jnp.concatenate([turned[c, pl.ds(at, WINDOW)] for c in range(4)], axis=0).astype(BF16)
        rows = [block_row(h, b, nbz) for b in range(blocks)]
        stack = []
        for part in (0, 48):
            piece = jnp.concatenate([tiles[row, part : part + 48] for row in rows], axis=1)
            stack += [piece, piece, jnp.concatenate([pad] * blocks, axis=1)]
        t = jnp.dot(jnp.concatenate([v, v], axis=1), jnp.concatenate(stack, axis=0), preferred_element_type=F32)
        for b, row in enumerate(rows):
            first, last = z_rows(b % GROUP)
            w, d = factors[row, 0, 0 : last - first], factors[row, 1, 0 : last - first]
            read = lambda c: t[WINDOW * c + first : WINDOW * c + last, 128 * b : 128 * b + 128]
            vz = read(2)
            for c, value in enumerate((w * read(0), w * read(1), w * vz, w * read(3) + d * vz)):
                sampled[c, pl.ds(row, 1), :] = jnp.sum(value, axis=0, keepdims=True)
        return carry

    lax.fori_loop(0, nbz // GROUP, group, 0, unroll=True)


def node_velocity(fields):
    mass = fields[0]
    inverse = 1.0 / jnp.maximum(mass, mass_floor)
    vel = [fields[k] * inverse for k in (1, 2, 3)]
    lifted = vel[2] - time_step * gravity
    floor = lax.broadcasted_iota(jnp.int32, lifted.shape, 2) == 0
    vel[2] = jnp.where(floor, jnp.maximum(lifted, 0.0), lifted)
    return mass, vel


def dragged(mass, vel, other_mass, other_vel, coef):
    slip = [b - a for a, b in zip(vel, other_vel)]
    rate = coef * jnp.sqrt(slip[0] * slip[0] + slip[1] * slip[1] + slip[2] * slip[2] + slip_floor)
    share = rate / (1.0 + rate) * (other_mass / (mass + other_mass + mass_floor))
    return [a + share * s for a, s in zip(vel, slip)]


class Side:
    def __init__(self):
        place_id = lax.axis_index("space")
        self.even = lax.rem(place_id, 2) == 0
        self.has_left = place_id > 0
        self.has_right = place_id < lax.axis_size("space") - 1

    def arrived(self, first, second, rows):
        first, second = first[rows], second[rows]
        from_left = jnp.where(self.even, second, first)
        from_right = jnp.where(self.even, first, second)
        return jnp.where(self.has_left, from_left, 0.0), jnp.where(self.has_right, from_right, 0.0)

    def layers(self, own, first, second):
        left, right = self.arrived(first, second, slice(0, 8))
        shape = (4, 2) + left.shape[1:]
        own = own[...]
        return jnp.concatenate(
            [own[:, 0:2] + left.reshape(shape), own[:, 2:4], own[:, 4:6] + right.reshape(shape)], axis=1
        )

    def send(self, own, first, second, coef=None):
        toward = jnp.where(self.even, 4, 0)
        for ref, start in ((first, toward), (second, 4 - toward)):
            for c in range(4):
                ref[2 * c : 2 * c + 2] = own[c, pl.ds(start, 2)]
        if coef is not None:
            first[8] = jnp.where(self.even, coef[3], coef[0])
            second[8] = jnp.where(self.even, coef[0], coef[3])

    def keep(self, vel):
        layer = lax.broadcasted_iota(jnp.int32, vel.shape, 0)
        keep = ((layer > 0) | self.has_left) & ((layer < vel.shape[0] - 1) | self.has_right)
        return jnp.where(keep, vel, 0.0)


def live_mask(count, shape):
    square = (shape[0], shape[0])
    same = lax.broadcasted_iota(jnp.int32, square, 0) == lax.broadcasted_iota(jnp.int32, square, 1)
    column = jnp.sum(jnp.where(same, count[...].astype(F32), 0.0), axis=1, keepdims=True)
    return lax.broadcasted_iota(jnp.int32, shape, 1).astype(F32) < column


def advance(sampled, kept, frac_ref, vel_ref, stress_ref):
    live = kept[LIVE] > 0.5
    vel = [sampled[k] for k in range(3)]
    rate = sampled[3] - kept[XC] * vel[0] - kept[YC] * vel[1]
    old = stress_ref[...]
    stress = jnp.where(live, old - (time_step * bulk_modulus * 4.0) * rate, old)
    frac = [jnp.where(live, frac_ref[k] + time_step * vel[k], frac_ref[k]) for k in range(3)]
    vel = [jnp.where(live, vel[k], vel_ref[k]) for k in range(3)]
    return frac, vel, stress


def store_state(state, new_frac, new_vel, new_stress):
    frac, vel, stress = state
    for k in range(3):
        new_frac[k] = frac[k]
        new_vel[k] = vel[k]
    new_stress[...] = stress


def first_kernel(sizes, *refs):
    sources, inputs, rest = refs[:7], refs[7:14], refs[14:]
    kept, tiles, factors, dep, first, second, planes, sums, sems = rest
    copies = [pltpu.make_async_copy(a, b, sems.at[k]) for k, (a, b) in enumerate(zip(sources, inputs))]
    for copy in copies:
        copy.start()
    for copy in copies:
        copy.wait()
    cell, count, frac, vel, mass, stress, coef = inputs
    live = live_mask(count, cell.shape)
    kept[LIVE] = jnp.where(live, 1.0, 0.0)
    m = jnp.where(live, mass[...], 0.0)
    s = jnp.where(live, stress[...], 0.0)
    prepare(cell[...], [frac[k] for k in range(3)], planes, kept, m, [vel[k] for k in range(3)], s, *sizes)
    deposit(planes, tiles, factors, sums, dep, *sizes)
    Side().send(dep, first, second, coef)


def total_kernel(dep, first, second, fields):
    fields[...] = Side().layers(dep, first, second)


def middle_kernel(sizes, cell, frac, vel, mass, stress, coef, kept, tiles, factors, fields, other, first, second,
                  new_frac, new_vel, new_stress, new_kept, new_tiles, new_factors, dep, new_first, new_second,
                  planes, sums, turned, sampled):
    side = Side()
    own_mass, own_vel = node_velocity(fields)
    other_mass, other_vel = node_velocity(other)
    low, high = side.arrived(first, second, slice(8, 9))
    coefs = jnp.concatenate([low, coef[...], high], axis=0)
    nodes = [side.keep(v) for v in dragged(own_mass, own_vel, other_mass, other_vel, coefs)]
    gather(nodes, tiles, factors, turned, sampled, *sizes)
    state = advance(sampled, kept, frac, vel, stress)
    store_state(state, new_frac, new_vel, new_stress)
    new_kept[LIVE] = kept[LIVE]
    live = kept[LIVE] > 0.5
    m = jnp.where(live, mass[...], 0.0)
    s = jnp.where(live, state[2], 0.0)
    prepare(cell[...], state[0], planes, new_kept, m, state[1], s, *sizes)
    deposit(planes, new_tiles, new_factors, sums, dep, *sizes)
    side.send(dep, new_first, new_second)


def last_kernel(sizes, frac, vel, stress, kept, tiles, factors, dep, first, second,
                new_frac, new_vel, new_stress, turned, sampled):
    side = Side()
    _, nodes = node_velocity(side.layers(dep, first, second))
    gather([side.keep(v) for v in nodes], tiles, factors, turned, sampled, *sizes)
    store_state(advance(sampled, kept, frac, vel, stress), new_frac, new_vel, new_stress)


def call(kernel, outs, scratch, *args, space=pltpu.VMEM, cost=None, limit=24 << 20):
    spec = pl.BlockSpec(memory_space=space)
    vmem = pl.BlockSpec(memory_space=pltpu.VMEM)
    return pl.pallas_call(
        kernel,
        out_shape=[jax.ShapeDtypeStruct(*(s if isinstance(s[0], tuple) else (s, F32))) for s in outs],
        in_specs=[spec] * len(args),
        out_specs=[vmem] * len(outs),
        scratch_shapes=scratch,
        cost_estimate=cost,
        compiler_params=pltpu.CompilerParams(vmem_limit_bytes=limit),
    )(*args)


def local(particle_cell, block_count, particle_frac, particle_vel, particle_mass, particle_stress, drag_coef):
    cell, count = particle_cell[0], block_count
    frac, vel = particle_frac[0], particle_vel[0]
    mass, stress = particle_mass[0], particle_stress[0]
    layers, ny, nz = drag_coef.shape
    sizes = nby, nbz = ny // 4, nz // 4
    blocks, slots = cell.shape
    places = lax.axis_size("space")

    def matching(start):
        pairs = [(i, i) for i in range(start)]
        for i in range(start, places - 1, 2):
            pairs += [(i, i + 1), (i + 1, i)]
        return pairs + [(i, i) for i in range(len(pairs), places)]

    swap = [(i, i ^ 1) for i in range(lax.axis_size("phase"))]
    particle = (blocks, slots)
    triple = (3,) + particle
    grid = (4, layers + 2, ny, nz)
    saved = [triple, ((blocks, 96, slots), BF16), (blocks, 2, 16, slots)]
    planes = pltpu.VMEM((PLANES,) + particle, F32)
    sums = pltpu.VMEM((CHANNELS, (layers + 2) * ny, nz), F32)
    turned = pltpu.VMEM((4, nz + 24, 128), F32)
    sampled = pltpu.VMEM((4,) + particle, F32)

    def exchange(first, second):
        second = lax.ppermute(second, "space", matching(1))
        first = lax.ppermute(first, "space", matching(0))
        return first, second

    inputs = (cell, count, frac, vel, mass, stress, drag_coef)
    sent = (9, ny, nz)
    *loaded, kept, tiles, factors, dep, first, second = call(
        functools.partial(first_kernel, sizes),
        [(a.shape, a.dtype) for a in inputs] + saved + [grid, sent, sent],
        [planes, sums, pltpu.SemaphoreType.DMA((7,))],
        *[pltpu.with_memory_space_constraint(a, pltpu.HBM) for a in inputs], space=pltpu.HBM)
    first, second = exchange(first, second)
    fields, = call(total_kernel, [grid], [], dep, first, second)
    other = lax.ppermute(fields, "phase", swap)
    sent = (8, ny, nz)
    frac, vel, stress, kept, tiles, factors, dep, first, second = call(
        functools.partial(middle_kernel, sizes),
        [triple, triple, particle] + saved + [grid, sent, sent],
        [planes, sums, turned, sampled],
        loaded[0], *loaded[2:], kept, tiles, factors, fields, other, first, second)
    first, second = exchange(first, second)
    frac, vel, stress = call(
        functools.partial(last_kernel, sizes), [triple, triple, particle], [turned, sampled],
        frac, vel, stress, kept, tiles, factors, dep, first, second)
    return frac[None], vel[None], stress[None]


def solution(mesh):
    in_specs = (
        P("phase", "space", None),
        P("phase", "space"),
        P("phase", None, "space", None),
        P("phase", None, "space", None),
        P("phase", "space", None),
        P("phase", "space", None),
        P("space", None, None),
    )
    out_specs = (
        P("phase", None, "space", None),
        P("phase", None, "space", None),
        P("phase", "space", None),
    )
    return jax.shard_map(local, mesh=mesh, in_specs=in_specs, out_specs=out_specs, check_vma=False)
```

```python
import functools

import jax
import jax.numpy as jnp
from jax import lax
from jax.experimental import pallas as pl
from jax.experimental.pallas import tpu as pltpu
from jax.sharding import PartitionSpec as P


time_step = 0.05
gravity = 1.0
bulk_modulus = 4.0
mass_floor = 0.25
slip_floor = 0.25

F32 = jnp.float32
BF16 = jnp.bfloat16

WX, YAT, WY, ZAT, WZ, DZ = 0, 6, 7, 10, 11, 14
CHANNEL = 17
PLANES = 22
XC, YC, LIVE = 0, 1, 2

GROUP = 4
WINDOW = 24
EDGE = 1
CHANNELS = 5


def spline(frac):
    r = frac - 0.5
    low, high = 0.5 - r, 0.5 + r
    w = (0.5 * low * low, 0.75 - r * r, 0.5 * high * high)
    d = ((-1.0 - r) * w[0], -r * w[1], (1.0 - r) * w[2])
    return w, d


def place(where_at, first, values):
    k = where_at - first
    out = jnp.where(k == 2.0, values[2], 0.0)
    out = jnp.where(k == 1.0, values[1], out)
    return jnp.where(k == 0.0, values[0], out)


def halves(value):
    high = value.astype(BF16)
    return high, (value - high.astype(F32)).astype(BF16)


def prepare_places(cell, frac, planes, kept, nby, nbz):
    wx, _ = spline(frac[0])
    wy, _ = spline(frac[1])
    wz, dz = spline(frac[2])
    at_x = (cell >> 4).astype(F32)
    at_y = ((cell >> 2) & 3).astype(F32)
    block = lax.broadcasted_iota(jnp.int32, cell.shape, 0)
    at_y = at_y + 4.0 * sum((block >= nbz * k).astype(F32) for k in range(1, nby))
    planes[YAT] = at_y
    planes[ZAT] = (cell & 3).astype(F32)
    for t in range(3):
        planes[WY + t] = wy[t]
        planes[WZ + t] = wz[t]
        planes[DZ + t] = dz[t]
    for x in range(6):
        planes[WX + x] = place(float(x), at_x, wx)
    kept[XC] = at_x + (frac[0] - 2.0)
    kept[YC] = at_y + (frac[1] - 2.0 * nby)


def prepare_channels(planes, kept, mass, vel, stress):
    scaled = (4.0 * time_step) * stress
    planes[CHANNEL] = mass
    planes[CHANNEL + 1] = mass * vel[0] - scaled * kept[XC]
    planes[CHANNEL + 2] = mass * vel[1] - scaled * kept[YC]
    planes[CHANNEL + 3] = mass * vel[2]
    planes[CHANNEL + 4] = scaled


def z_rows(q):
    return 4 * q // 8 * 8, (4 * q + 5) // 8 * 8 + 8


def block_row(h, b, nbz):
    return b // GROUP * nbz + h * GROUP + b % GROUP


def deposit(planes, tiles, factors, sums, out, nby, nbz):
    sums[...] = jnp.zeros_like(sums)
    blocks = nby * GROUP

    def group(h, carry):
        columns, lines = [], []
        for b in range(blocks):
            row, q = block_row(h, b, nbz), b % GROUP
            get = lambda k: planes[k, pl.ds(row, 8, stride=0), :]
            at = lax.broadcasted_iota(jnp.int32, (8, 128), 0).astype(F32)
            wy = place(at, get(YAT) - 1.0, [get(WY + t) for t in range(3)])
            pieces = []
            for x in range(0, 6, 2):
                high, low = halves(jnp.concatenate([get(WX + x) * wy, get(WX + x + 1) * wy], axis=0))
                tiles[row, 8 * x : 8 * x + 16] = high
                tiles[row, 48 + 8 * x : 64 + 8 * x] = low
                pieces.append((high, low))
            lines.append(jnp.concatenate([p[0] for p in pieces] + [p[1] for p in pieces], axis=0))
            first, last = z_rows(q)
            steps = (last - first) // 8
            get = lambda k: jnp.concatenate([planes[k, pl.ds(row, 8, stride=0), :]] * steps, axis=0)
            at = lax.broadcasted_iota(jnp.int32, (last - first, 128), 0).astype(F32)
            start = get(ZAT) + float(4 * q - first)
            wz = place(at, start, [get(WZ + t) for t in range(3)])
            dz = place(at, start, [get(DZ + t) for t in range(3)])
            factors[row, 0, 0 : last - first] = wz
            factors[row, 1, 0 : last - first] = dz
            parts = [get(CHANNEL + c) * wz for c in range(CHANNELS)]
            parts[3] = parts[3] + get(CHANNEL + 4) * dz
            zeros = lambda n: [jnp.zeros((n, 128), F32)] if n else []
            high = [part.astype(BF16).astype(F32) for part in parts]
            low = [part - h for part, h in zip(parts, high)]
            stack = []
            for values in (high, low):
                for value in values:
                    stack += zeros(first) + [value] + zeros(WINDOW - last)
                stack += zeros(128 - CHANNELS * WINDOW)
            columns.append(jnp.concatenate(stack, axis=0).astype(BF16))
        a = jnp.concatenate(lines, axis=1)
        o = lax.dot_general(a, jnp.concatenate(columns, axis=1), (((1,), (1,)), ((), ())),
                            preferred_element_type=F32)
        o = o[0:48] + o[48:96]
        o = o[:, 0:128] + o[:, 128:256]
        z = lax.broadcasted_iota(jnp.int32, o.shape, 1) - (4 * GROUP * h - EDGE)
        inside = (z >= 0) & (z < WINDOW)
        for c in range(CHANNELS):
            moved = pltpu.roll(o, lax.rem(4 * GROUP * h + (128 - EDGE + 128 - WINDOW * c), 128), 1)
            sums[c] += jnp.where(inside, moved, 0.0)
        return carry

    lax.fori_loop(0, nbz // GROUP, group, 0, unroll=True)
    shape = out.shape[1:]
    x = lax.broadcasted_iota(jnp.int32, shape, 0).astype(F32) - 2.5
    y = lax.broadcasted_iota(jnp.int32, shape, 1).astype(F32) + (0.5 - 2.0 * nby)
    mass, mx, my, mz, stress = (sums[c].reshape(shape) for c in range(CHANNELS))
    out[0] = mass
    out[1] = mx + x * stress
    out[2] = my + y * stress
    out[3] = mz


def gather(vel, tiles, factors, turned, sampled, nby, nbz, ready=None):
    parts = 1 if ready is None else nby
    blocks = nby // parts * GROUP
    shape = vel[0].shape
    x = lax.broadcasted_iota(jnp.int32, shape, 0).astype(F32) - 2.5
    y = lax.broadcasted_iota(jnp.int32, shape, 1).astype(F32) + (0.5 - 2.0 * nby)
    for c, v in enumerate((vel[0], vel[1], vel[2], x * vel[0] + y * vel[1])):
        v = v.reshape(48, 128)
        high = v.astype(BF16).astype(F32)
        v = jnp.concatenate([high, v - high, jnp.zeros((32, 128), F32)], axis=0)
        turned[c, 0:8] = jnp.zeros((8, 128), F32)
        turned[c, 128:152] = jnp.zeros((24, 128), F32)
        turned[c, EDGE : EDGE + 128] = v.T
    pad = jnp.zeros((32, 128), F32).astype(BF16)

    def group(h, part):
        at = pl.multiple_of(4 * GROUP * h, 8)
        v = jnp.concatenate([turned[c, pl.ds(at, WINDOW)] for c in range(4)], axis=0).astype(BF16)
        rows = [part * nbz + block_row(h, b, nbz) for b in range(blocks)]
        stack = []
        for half in (0, 48):
            piece = jnp.concatenate([tiles[row, half : half + 48] for row in rows], axis=1)
            stack += [piece, piece, jnp.concatenate([pad] * blocks, axis=1)]
        t = jnp.dot(jnp.concatenate([v, v], axis=1), jnp.concatenate(stack, axis=0), preferred_element_type=F32)
        for b, row in enumerate(rows):
            first, last = z_rows(b % GROUP)
            w, d = factors[row, 0, 0 : last - first], factors[row, 1, 0 : last - first]
            read = lambda c: t[WINDOW * c + first : WINDOW * c + last, 128 * b : 128 * b + 128]
            vz = read(2)
            for c, value in enumerate((w * read(0), w * read(1), w * vz, w * read(3) + d * vz)):
                sampled[c, pl.ds(row, 1), :] = jnp.sum(value, axis=0, keepdims=True)
        return part

    for part in range(parts):
        lax.fori_loop(0, nbz // GROUP, group, part, unroll=True)
        if ready is not None:
            ready(pl.ds(part * nbz, nbz))


def node_velocity(fields):
    mass = fields[0]
    inverse = 1.0 / jnp.maximum(mass, mass_floor)
    vel = [fields[k] * inverse for k in (1, 2, 3)]
    lifted = vel[2] - time_step * gravity
    floor = lax.broadcasted_iota(jnp.int32, lifted.shape, 2) == 0
    vel[2] = jnp.where(floor, jnp.maximum(lifted, 0.0), lifted)
    return mass, vel


def dragged(mass, vel, other_mass, other_vel, coef):
    slip = [b - a for a, b in zip(vel, other_vel)]
    rate = coef * jnp.sqrt(slip[0] * slip[0] + slip[1] * slip[1] + slip[2] * slip[2] + slip_floor)
    share = rate / (1.0 + rate) * (other_mass / (mass + other_mass + mass_floor))
    return [a + share * s for a, s in zip(vel, slip)]


class Side:
    def __init__(self):
        place_id = lax.axis_index("space")
        self.even = lax.rem(place_id, 2) == 0
        self.has_left = place_id > 0
        self.has_right = place_id < lax.axis_size("space") - 1

    def arrived(self, first, second, rows):
        first, second = first[rows], second[rows]
        from_left = jnp.where(self.even, second, first)
        from_right = jnp.where(self.even, first, second)
        return jnp.where(self.has_left, from_left, 0.0), jnp.where(self.has_right, from_right, 0.0)

    def layers(self, own, first, second):
        left, right = self.arrived(first, second, slice(0, 8))
        shape = (4, 2) + left.shape[1:]
        own = own[...]
        return jnp.concatenate(
            [own[:, 0:2] + left.reshape(shape), own[:, 2:4], own[:, 4:6] + right.reshape(shape)], axis=1
        )

    def send(self, own, first, second, coef=None):
        toward = jnp.where(self.even, 4, 0)
        for ref, start in ((first, toward), (second, 4 - toward)):
            for c in range(4):
                ref[2 * c : 2 * c + 2] = own[c, pl.ds(start, 2)]
        if coef is not None:
            first[8] = jnp.where(self.even, coef[3], coef[0])
            second[8] = jnp.where(self.even, coef[0], coef[3])

    def keep(self, vel):
        layer = lax.broadcasted_iota(jnp.int32, vel.shape, 0)
        keep = ((layer > 0) | self.has_left) & ((layer < vel.shape[0] - 1) | self.has_right)
        return jnp.where(keep, vel, 0.0)


def live_mask(count, shape):
    square = (shape[0], shape[0])
    same = lax.broadcasted_iota(jnp.int32, square, 0) == lax.broadcasted_iota(jnp.int32, square, 1)
    column = jnp.sum(jnp.where(same, count[...].astype(F32), 0.0), axis=1, keepdims=True)
    return lax.broadcasted_iota(jnp.int32, shape, 1).astype(F32) < column


def advance(sampled, kept, frac_ref, vel_ref, stress_ref, rows=slice(None)):
    live = kept[LIVE, rows] > 0.5
    vel = [sampled[k, rows] for k in range(3)]
    rate = sampled[3, rows] - kept[XC, rows] * vel[0] - kept[YC, rows] * vel[1]
    old = stress_ref[rows]
    stress = jnp.where(live, old - (time_step * bulk_modulus * 4.0) * rate, old)
    frac = [jnp.where(live, frac_ref[k, rows] + time_step * vel[k], frac_ref[k, rows]) for k in range(3)]
    vel = [jnp.where(live, vel[k], vel_ref[k, rows]) for k in range(3)]
    return frac, vel, stress


def store_state(state, new_frac, new_vel, new_stress, rows=slice(None)):
    frac, vel, stress = state
    for k in range(3):
        new_frac[k, rows] = frac[k]
        new_vel[k, rows] = vel[k]
    new_stress[rows] = stress


def first_kernel(sizes, *refs):
    sources, inputs, rest = refs[:7], refs[7:14], refs[14:]
    kept, tiles, factors, dep, first, second, planes, sums, sems = rest
    copies = [pltpu.make_async_copy(a, b, sems.at[k]) for k, (a, b) in enumerate(zip(sources, inputs))]
    cell, count, frac, vel, mass, stress, coef = inputs
    for k in (2, 0, 1, 4, 5, 3, 6):
        copies[k].start()
    copies[2].wait()
    copies[0].wait()
    prepare_places(cell[...], [frac[k] for k in range(3)], planes, kept, *sizes)
    for k in (1, 4, 5, 3):
        copies[k].wait()
    live = live_mask(count, cell.shape)
    kept[LIVE] = jnp.where(live, 1.0, 0.0)
    m = jnp.where(live, mass[...], 0.0)
    s = jnp.where(live, stress[...], 0.0)
    prepare_channels(planes, kept, m, [vel[k] for k in range(3)], s)
    deposit(planes, tiles, factors, sums, dep, *sizes)
    copies[6].wait()
    Side().send(dep, first, second, coef)


def total_kernel(dep, first, second, fields):
    fields[...] = Side().layers(dep, first, second)


def middle_kernel(sizes, cell, frac, vel, mass, stress, coef, kept, tiles, factors, fields, other, first, second,
                  new_frac, new_vel, new_stress, new_kept, new_tiles, new_factors, dep, new_first, new_second,
                  planes, sums, turned, sampled):
    side = Side()
    own_mass, own_vel = node_velocity(fields)
    other_mass, other_vel = node_velocity(other)
    low, high = side.arrived(first, second, slice(8, 9))
    coefs = jnp.concatenate([low, coef[...], high], axis=0)
    nodes = [side.keep(v) for v in dragged(own_mass, own_vel, other_mass, other_vel, coefs)]
    gather(nodes, tiles, factors, turned, sampled, *sizes)
    state = advance(sampled, kept, frac, vel, stress)
    store_state(state, new_frac, new_vel, new_stress)
    new_kept[LIVE] = kept[LIVE]
    live = kept[LIVE] > 0.5
    m = jnp.where(live, mass[...], 0.0)
    s = jnp.where(live, state[2], 0.0)
    prepare_places(cell[...], state[0], planes, new_kept, *sizes)
    prepare_channels(planes, new_kept, m, state[1], s)
    deposit(planes, new_tiles, new_factors, sums, dep, *sizes)
    side.send(dep, new_first, new_second)


def last_kernel(sizes, frac, vel, stress, kept, tiles, factors, dep, first, second,
                frac_out, vel_out, stress_out, new_frac, new_vel, new_stress, turned, sampled, sems):
    side = Side()
    copies = []

    def ready(rows):
        store_state(advance(sampled, kept, frac, vel, stress, rows), new_frac, new_vel, new_stress, rows)
        pairs = (
            (new_frac.at[:, rows], frac_out.at[:, rows]),
            (new_vel.at[:, rows], vel_out.at[:, rows]),
            (new_stress.at[rows], stress_out.at[rows]),
        )
        for source, target in pairs:
            copy = pltpu.make_async_copy(source, target, sems.at[len(copies)])
            copy.start()
            copies.append(copy)

    _, nodes = node_velocity(side.layers(dep, first, second))
    gather([side.keep(v) for v in nodes], tiles, factors, turned, sampled, *sizes, ready)
    for copy in copies:
        copy.wait()


def call(kernel, outs, scratch, *args, space=pltpu.VMEM, out_space=pltpu.VMEM):
    spec = pl.BlockSpec(memory_space=space)
    out_spec = pl.BlockSpec(memory_space=out_space)
    return pl.pallas_call(
        kernel,
        out_shape=[jax.ShapeDtypeStruct(*(s if isinstance(s[0], tuple) else (s, F32))) for s in outs],
        in_specs=[spec] * len(args),
        out_specs=[out_spec] * len(outs),
        scratch_shapes=scratch,
        compiler_params=pltpu.CompilerParams(vmem_limit_bytes=24 << 20),
    )(*args)


def local(particle_cell, block_count, particle_frac, particle_vel, particle_mass, particle_stress, drag_coef):
    cell, count = particle_cell[0], block_count
    frac, vel = particle_frac[0], particle_vel[0]
    mass, stress = particle_mass[0], particle_stress[0]
    layers, ny, nz = drag_coef.shape
    sizes = nby, nbz = ny // 4, nz // 4
    blocks, slots = cell.shape
    places = lax.axis_size("space")

    def matching(start):
        pairs = [(i, i) for i in range(start)]
        for i in range(start, places - 1, 2):
            pairs += [(i, i + 1), (i + 1, i)]
        return pairs + [(i, i) for i in range(len(pairs), places)]

    swap = [(i, i ^ 1) for i in range(lax.axis_size("phase"))]
    particle = (blocks, slots)
    triple = (3,) + particle
    grid = (4, layers + 2, ny, nz)
    saved = [triple, ((blocks, 96, slots), BF16), (blocks, 2, 16, slots)]
    planes = pltpu.VMEM((PLANES,) + particle, F32)
    sums = pltpu.VMEM((CHANNELS, (layers + 2) * ny, nz), F32)
    turned = pltpu.VMEM((4, nz + 24, 128), F32)
    sampled = pltpu.VMEM((4,) + particle, F32)

    def exchange(first, second):
        second = lax.ppermute(second, "space", matching(1))
        first = lax.ppermute(first, "space", matching(0))
        return first, second

    inputs = (cell, count, frac, vel, mass, stress, drag_coef)
    sent = (9, ny, nz)
    *loaded, kept, tiles, factors, dep, first, second = call(
        functools.partial(first_kernel, sizes),
        [(a.shape, a.dtype) for a in inputs] + saved + [grid, sent, sent],
        [planes, sums, pltpu.SemaphoreType.DMA((7,))],
        *[pltpu.with_memory_space_constraint(a, pltpu.HBM) for a in inputs], space=pltpu.HBM)
    first, second = exchange(first, second)
    fields, = call(total_kernel, [grid], [], dep, first, second)
    other = lax.ppermute(fields, "phase", swap)
    sent = (8, ny, nz)
    frac, vel, stress, kept, tiles, factors, dep, first, second = call(
        functools.partial(middle_kernel, sizes),
        [triple, triple, particle] + saved + [grid, sent, sent],
        [planes, sums, turned, sampled],
        loaded[0], *loaded[2:], kept, tiles, factors, fields, other, first, second)
    first, second = exchange(first, second)
    frac, vel, stress = call(
        functools.partial(last_kernel, sizes), [triple, triple, particle],
        [pltpu.VMEM(a.shape, F32) for a in (frac, vel, stress)]
        + [turned, sampled, pltpu.SemaphoreType.DMA((3 * nby,))],
        frac, vel, stress, kept, tiles, factors, dep, first, second, out_space=pl.ANY)
    return frac[None], vel[None], stress[None]


def solution(mesh):
    in_specs = (
        P("phase", "space", None),
        P("phase", "space"),
        P("phase", None, "space", None),
        P("phase", None, "space", None),
        P("phase", "space", None),
        P("phase", "space", None),
        P("space", None, None),
    )
    out_specs = (
        P("phase", None, "space", None),
        P("phase", None, "space", None),
        P("phase", "space", None),
    )
    return jax.shard_map(local, mesh=mesh, in_specs=in_specs, out_specs=out_specs, check_vma=False)
```

```python
import functools

import jax
import jax.numpy as jnp
from jax import lax
from jax.experimental import pallas as pl
from jax.experimental.pallas import tpu as pltpu
from jax.sharding import PartitionSpec as P


time_step = 0.05
gravity = 1.0
bulk_modulus = 4.0
mass_floor = 0.25
slip_floor = 0.25

F32 = jnp.float32
BF16 = jnp.bfloat16

WX, YAT, WY, ZAT, WZ, DZ = 0, 6, 7, 10, 11, 14
CHANNEL = 17
PLANES = 22
XC, YC, LIVE = 0, 1, 2

GROUP = 4
WINDOW = 24
EDGE = 1
CHANNELS = 5


def spline(frac):
    r = frac - 0.5
    low, high = 0.5 - r, 0.5 + r
    w = (0.5 * low * low, 0.75 - r * r, 0.5 * high * high)
    d = ((-1.0 - r) * w[0], -r * w[1], (1.0 - r) * w[2])
    return w, d


def place(where_at, first, values):
    k = where_at - first
    out = jnp.where(k == 2.0, values[2], 0.0)
    out = jnp.where(k == 1.0, values[1], out)
    return jnp.where(k == 0.0, values[0], out)


def halves(value):
    high = value.astype(BF16)
    return high, (value - high.astype(F32)).astype(BF16)


def prepare(cell, frac, planes, kept, mass, vel, stress, nby, nbz):
    wx, _ = spline(frac[0])
    wy, _ = spline(frac[1])
    wz, dz = spline(frac[2])
    at_x = (cell >> 4).astype(F32)
    at_y = ((cell >> 2) & 3).astype(F32)
    block = lax.broadcasted_iota(jnp.int32, cell.shape, 0)
    at_y = at_y + 4.0 * sum((block >= nbz * k).astype(F32) for k in range(1, nby))
    planes[YAT] = at_y
    planes[ZAT] = (cell & 3).astype(F32)
    for t in range(3):
        planes[WY + t] = wy[t]
        planes[WZ + t] = wz[t]
        planes[DZ + t] = dz[t]
    for x in range(6):
        planes[WX + x] = place(float(x), at_x, wx)
    position = (at_x + (frac[0] - 2.0), at_y + (frac[1] - 2.0 * nby))
    kept[XC] = position[0]
    kept[YC] = position[1]
    scaled = (4.0 * time_step) * stress
    planes[CHANNEL] = mass
    planes[CHANNEL + 1] = mass * vel[0] - scaled * position[0]
    planes[CHANNEL + 2] = mass * vel[1] - scaled * position[1]
    planes[CHANNEL + 3] = mass * vel[2]
    planes[CHANNEL + 4] = scaled


def z_rows(q):
    return 4 * q // 8 * 8, (4 * q + 5) // 8 * 8 + 8


def block_row(h, b, nbz):
    return b // GROUP * nbz + h * GROUP + b % GROUP


def deposit(planes, tiles, factors, sums, out, nby, nbz):
    sums[...] = jnp.zeros_like(sums)
    blocks = nby * GROUP

    def group(h, carry):
        columns, lines = [], []
        for b in range(blocks):
            row, q = block_row(h, b, nbz), b % GROUP
            get = lambda k: planes[k, pl.ds(row, 8, stride=0), :]
            at = lax.broadcasted_iota(jnp.int32, (8, 128), 0).astype(F32)
            wy = place(at, get(YAT) - 1.0, [get(WY + t) for t in range(3)])
            pieces = []
            for x in range(0, 6, 2):
                high, low = halves(jnp.concatenate([get(WX + x) * wy, get(WX + x + 1) * wy], axis=0))
                tiles[row, 8 * x : 8 * x + 16] = high
                tiles[row, 48 + 8 * x : 64 + 8 * x] = low
                pieces.append((high, low))
            lines.append(jnp.concatenate([p[0] for p in pieces] + [p[1] for p in pieces], axis=0))
            first, last = z_rows(q)
            steps = (last - first) // 8
            get = lambda k: jnp.concatenate([planes[k, pl.ds(row, 8, stride=0), :]] * steps, axis=0)
            at = lax.broadcasted_iota(jnp.int32, (last - first, 128), 0).astype(F32)
            start = get(ZAT) + float(4 * q - first)
            wz = place(at, start, [get(WZ + t) for t in range(3)])
            dz = place(at, start, [get(DZ + t) for t in range(3)])
            factors[row, 0, 0 : last - first] = wz
            factors[row, 1, 0 : last - first] = dz
            parts = [get(CHANNEL + c) * wz for c in range(CHANNELS)]
            parts[3] = parts[3] + get(CHANNEL + 4) * dz
            zeros = lambda n: [jnp.zeros((n, 128), F32)] if n else []
            high = [part.astype(BF16).astype(F32) for part in parts]
            low = [part - h for part, h in zip(parts, high)]
            stack = []
            for values in (high, low):
                for value in values:
                    stack += zeros(first) + [value] + zeros(WINDOW - last)
                stack += zeros(128 - CHANNELS * WINDOW)
            columns.append(jnp.concatenate(stack, axis=0).astype(BF16))
        a = jnp.concatenate(lines, axis=1)
        o = lax.dot_general(a, jnp.concatenate(columns, axis=1), (((1,), (1,)), ((), ())),
                            preferred_element_type=F32)
        o = o[0:48] + o[48:96]
        o = o[:, 0:128] + o[:, 128:256]
        z = lax.broadcasted_iota(jnp.int32, o.shape, 1) - (4 * GROUP * h - EDGE)
        inside = (z >= 0) & (z < WINDOW)
        for c in range(CHANNELS):
            moved = pltpu.roll(o, lax.rem(4 * GROUP * h + (128 - EDGE + 128 - WINDOW * c), 128), 1)
            sums[c] += jnp.where(inside, moved, 0.0)
        return carry

    lax.fori_loop(0, nbz // GROUP, group, 0, unroll=True)
    shape = out.shape[1:]
    x = lax.broadcasted_iota(jnp.int32, shape, 0).astype(F32) - 2.5
    y = lax.broadcasted_iota(jnp.int32, shape, 1).astype(F32) + (0.5 - 2.0 * nby)
    mass, mx, my, mz, stress = (sums[c].reshape(shape) for c in range(CHANNELS))
    out[0] = mass
    out[1] = mx + x * stress
    out[2] = my + y * stress
    out[3] = mz


def gather(vel, tiles, factors, turned, sampled, nby, nbz):
    blocks = nby * GROUP
    shape = vel[0].shape
    x = lax.broadcasted_iota(jnp.int32, shape, 0).astype(F32) - 2.5
    y = lax.broadcasted_iota(jnp.int32, shape, 1).astype(F32) + (0.5 - 2.0 * nby)
    for c, v in enumerate((vel[0], vel[1], vel[2], x * vel[0] + y * vel[1])):
        v = v.reshape(48, 128)
        high = v.astype(BF16).astype(F32)
        v = jnp.concatenate([high, v - high, jnp.zeros((32, 128), F32)], axis=0)
        turned[c, 0:8] = jnp.zeros((8, 128), F32)
        turned[c, 128:152] = jnp.zeros((24, 128), F32)
        turned[c, EDGE : EDGE + 128] = v.T
    pad = jnp.zeros((32, 128), F32).astype(BF16)

    def group(h, carry):
        at = pl.multiple_of(4 * GROUP * h, 8)
        v = jnp.concatenate([turned[c, pl.ds(at, WINDOW)] for c in range(4)], axis=0).astype(BF16)
        rows = [block_row(h, b, nbz) for b in range(blocks)]
        stack = []
        for part in (0, 48):
            piece = jnp.concatenate([tiles[row, part : part + 48] for row in rows], axis=1)
            stack += [piece, piece, jnp.concatenate([pad] * blocks, axis=1)]
        t = jnp.dot(jnp.concatenate([v, v], axis=1), jnp.concatenate(stack, axis=0), preferred_element_type=F32)
        for b, row in enumerate(rows):
            first, last = z_rows(b % GROUP)
            w, d = factors[row, 0, 0 : last - first], factors[row, 1, 0 : last - first]
            read = lambda c: t[WINDOW * c + first : WINDOW * c + last, 128 * b : 128 * b + 128]
            vz = read(2)
            for c, value in enumerate((w * read(0), w * read(1), w * vz, w * read(3) + d * vz)):
                sampled[c, pl.ds(row, 1), :] = jnp.sum(value, axis=0, keepdims=True)
        return carry

    lax.fori_loop(0, nbz // GROUP, group, 0, unroll=True)


def node_velocity(fields):
    mass = fields[0]
    inverse = 1.0 / jnp.maximum(mass, mass_floor)
    vel = [fields[k] * inverse for k in (1, 2, 3)]
    lifted = vel[2] - time_step * gravity
    floor = lax.broadcasted_iota(jnp.int32, lifted.shape, 2) == 0
    vel[2] = jnp.where(floor, jnp.maximum(lifted, 0.0), lifted)
    return mass, vel


def dragged(mass, vel, other_mass, other_vel, coef):
    slip = [b - a for a, b in zip(vel, other_vel)]
    rate = coef * jnp.sqrt(slip[0] * slip[0] + slip[1] * slip[1] + slip[2] * slip[2] + slip_floor)
    share = rate / (1.0 + rate) * (other_mass / (mass + other_mass + mass_floor))
    return [a + share * s for a, s in zip(vel, slip)]


class Side:
    def __init__(self):
        place_id = lax.axis_index("space")
        self.even = lax.rem(place_id, 2) == 0
        self.has_left = place_id > 0
        self.has_right = place_id < lax.axis_size("space") - 1

    def arrived(self, first, second, rows):
        first, second = first[rows], second[rows]
        from_left = jnp.where(self.even, second, first)
        from_right = jnp.where(self.even, first, second)
        return jnp.where(self.has_left, from_left, 0.0), jnp.where(self.has_right, from_right, 0.0)

    def layers(self, own, first, second):
        left, right = self.arrived(first, second, slice(0, 8))
        shape = (4, 2) + left.shape[1:]
        own = own[...]
        return jnp.concatenate(
            [own[:, 0:2] + left.reshape(shape), own[:, 2:4], own[:, 4:6] + right.reshape(shape)], axis=1
        )

    def send(self, own, first, second, coef=None):
        toward = jnp.where(self.even, 4, 0)
        for ref, start in ((first, toward), (second, 4 - toward)):
            for c in range(4):
                ref[2 * c : 2 * c + 2] = own[c, pl.ds(start, 2)]
        if coef is not None:
            first[8] = jnp.where(self.even, coef[3], coef[0])
            second[8] = jnp.where(self.even, coef[0], coef[3])

    def keep(self, vel):
        layer = lax.broadcasted_iota(jnp.int32, vel.shape, 0)
        keep = ((layer > 0) | self.has_left) & ((layer < vel.shape[0] - 1) | self.has_right)
        return jnp.where(keep, vel, 0.0)


def live_mask(count, shape):
    square = (shape[0], shape[0])
    same = lax.broadcasted_iota(jnp.int32, square, 0) == lax.broadcasted_iota(jnp.int32, square, 1)
    column = jnp.sum(jnp.where(same, count[...].astype(F32), 0.0), axis=1, keepdims=True)
    return lax.broadcasted_iota(jnp.int32, shape, 1).astype(F32) < column


def advance(sampled, kept, frac_ref, vel_ref, stress_ref):
    live = kept[LIVE] > 0.5
    vel = [sampled[k] for k in range(3)]
    rate = sampled[3] - kept[XC] * vel[0] - kept[YC] * vel[1]
    old = stress_ref[...]
    stress = jnp.where(live, old - (time_step * bulk_modulus * 4.0) * rate, old)
    frac = [jnp.where(live, frac_ref[k] + time_step * vel[k], frac_ref[k]) for k in range(3)]
    vel = [jnp.where(live, vel[k], vel_ref[k]) for k in range(3)]
    return frac, vel, stress


def store_state(state, new_frac, new_vel, new_stress):
    frac, vel, stress = state
    for k in range(3):
        new_frac[k] = frac[k]
        new_vel[k] = vel[k]
    new_stress[...] = stress


def first_kernel(sizes, *refs):
    sources, inputs, rest = refs[:7], refs[7:14], refs[14:]
    kept, tiles, factors, dep, first, second, planes, sums, sems = rest
    pairs = []
    for a, b in zip(sources, inputs):
        split = len(a.shape) == 3
        pairs += [(a.at[k], b.at[k]) for k in range(a.shape[0])] if split else [(a, b)]
    copies = [pltpu.make_async_copy(a, b, sems.at[k]) for k, (a, b) in enumerate(pairs)]
    for copy in copies:
        copy.start()
    for copy in copies:
        copy.wait()
    cell, count, frac, vel, mass, stress, coef = inputs
    live = live_mask(count, cell.shape)
    kept[LIVE] = jnp.where(live, 1.0, 0.0)
    m = jnp.where(live, mass[...], 0.0)
    s = jnp.where(live, stress[...], 0.0)
    prepare(cell[...], [frac[k] for k in range(3)], planes, kept, m, [vel[k] for k in range(3)], s, *sizes)
    deposit(planes, tiles, factors, sums, dep, *sizes)
    Side().send(dep, first, second, coef)


def total_kernel(dep, first, second, fields):
    fields[...] = Side().layers(dep, first, second)


def middle_kernel(sizes, cell, frac, vel, mass, stress, coef, kept, tiles, factors, fields, other, first, second,
                  new_frac, new_vel, new_stress, new_kept, new_tiles, new_factors, dep, new_first, new_second,
                  planes, sums, turned, sampled):
    side = Side()
    own_mass, own_vel = node_velocity(fields)
    other_mass, other_vel = node_velocity(other)
    low, high = side.arrived(first, second, slice(8, 9))
    coefs = jnp.concatenate([low, coef[...], high], axis=0)
    nodes = [side.keep(v) for v in dragged(own_mass, own_vel, other_mass, other_vel, coefs)]
    gather(nodes, tiles, factors, turned, sampled, *sizes)
    state = advance(sampled, kept, frac, vel, stress)
    store_state(state, new_frac, new_vel, new_stress)
    new_kept[LIVE] = kept[LIVE]
    live = kept[LIVE] > 0.5
    m = jnp.where(live, mass[...], 0.0)
    s = jnp.where(live, state[2], 0.0)
    prepare(cell[...], state[0], planes, new_kept, m, state[1], s, *sizes)
    deposit(planes, new_tiles, new_factors, sums, dep, *sizes)
    side.send(dep, new_first, new_second)


def last_kernel(sizes, frac, vel, stress, kept, tiles, factors, dep, first, second,
                new_frac, new_vel, new_stress, turned, sampled):
    side = Side()
    _, nodes = node_velocity(side.layers(dep, first, second))
    gather([side.keep(v) for v in nodes], tiles, factors, turned, sampled, *sizes)
    store_state(advance(sampled, kept, frac, vel, stress), new_frac, new_vel, new_stress)


def call(kernel, outs, scratch, *args, space=pltpu.VMEM, cost=None, limit=24 << 20):
    spec = pl.BlockSpec(memory_space=space)
    vmem = pl.BlockSpec(memory_space=pltpu.VMEM)
    return pl.pallas_call(
        kernel,
        out_shape=[jax.ShapeDtypeStruct(*(s if isinstance(s[0], tuple) else (s, F32))) for s in outs],
        in_specs=[spec] * len(args),
        out_specs=[vmem] * len(outs),
        scratch_shapes=scratch,
        cost_estimate=cost,
        compiler_params=pltpu.CompilerParams(vmem_limit_bytes=limit),
    )(*args)


def local(particle_cell, block_count, particle_frac, particle_vel, particle_mass, particle_stress, drag_coef):
    cell, count = particle_cell[0], block_count
    frac, vel = particle_frac[0], particle_vel[0]
    mass, stress = particle_mass[0], particle_stress[0]
    layers, ny, nz = drag_coef.shape
    sizes = nby, nbz = ny // 4, nz // 4
    blocks, slots = cell.shape
    places = lax.axis_size("space")

    def matching(start):
        pairs = [(i, i) for i in range(start)]
        for i in range(start, places - 1, 2):
            pairs += [(i, i + 1), (i + 1, i)]
        return pairs + [(i, i) for i in range(len(pairs), places)]

    swap = [(i, i ^ 1) for i in range(lax.axis_size("phase"))]
    particle = (blocks, slots)
    triple = (3,) + particle
    grid = (4, layers + 2, ny, nz)
    saved = [triple, ((blocks, 96, slots), BF16), (blocks, 2, 16, slots)]
    planes = pltpu.VMEM((PLANES,) + particle, F32)
    sums = pltpu.VMEM((CHANNELS, (layers + 2) * ny, nz), F32)
    turned = pltpu.VMEM((4, nz + 24, 128), F32)
    sampled = pltpu.VMEM((4,) + particle, F32)

    def exchange(first, second):
        second = lax.ppermute(second, "space", matching(1))
        first = lax.ppermute(first, "space", matching(0))
        return first, second

    inputs = (cell, count, frac, vel, mass, stress, drag_coef)
    sent = (9, ny, nz)
    *loaded, kept, tiles, factors, dep, first, second = call(
        functools.partial(first_kernel, sizes),
        [(a.shape, a.dtype) for a in inputs] + saved + [grid, sent, sent],
        [planes, sums, pltpu.SemaphoreType.DMA((10 + layers,))],
        *[pltpu.with_memory_space_constraint(a, pltpu.HBM) for a in inputs], space=pltpu.HBM)
    first, second = exchange(first, second)
    fields, = call(total_kernel, [grid], [], dep, first, second)
    other = lax.ppermute(fields, "phase", swap)
    sent = (8, ny, nz)
    frac, vel, stress, kept, tiles, factors, dep, first, second = call(
        functools.partial(middle_kernel, sizes),
        [triple, triple, particle] + saved + [grid, sent, sent],
        [planes, sums, turned, sampled],
        loaded[0], *loaded[2:], kept, tiles, factors, fields, other, first, second)
    first, second = exchange(first, second)
    frac, vel, stress = call(
        functools.partial(last_kernel, sizes), [triple, triple, particle], [turned, sampled],
        frac, vel, stress, kept, tiles, factors, dep, first, second)
    return frac[None], vel[None], stress[None]


def solution(mesh):
    in_specs = (
        P("phase", "space", None),
        P("phase", "space"),
        P("phase", None, "space", None),
        P("phase", None, "space", None),
        P("phase", "space", None),
        P("phase", "space", None),
        P("space", None, None),
    )
    out_specs = (
        P("phase", None, "space", None),
        P("phase", None, "space", None),
        P("phase", "space", None),
    )
    return jax.shard_map(local, mesh=mesh, in_specs=in_specs, out_specs=out_specs, check_vma=False)
```

```python
import functools

import jax
import jax.numpy as jnp
from jax import lax
from jax.experimental import pallas as pl
from jax.experimental.pallas import tpu as pltpu
from jax.sharding import PartitionSpec as P


time_step = 0.05
gravity = 1.0
bulk_modulus = 4.0
mass_floor = 0.25
slip_floor = 0.25

F32 = jnp.float32
BF16 = jnp.bfloat16

WX, YAT, WY, ZAT, WZ, DZ = 0, 6, 7, 10, 11, 14
CHANNEL = 17
PLANES = 22
XC, YC, LIVE = 0, 1, 2

GROUP = 4
WINDOW = 24
EDGE = 1
CHANNELS = 5


def spline(frac):
    r = frac - 0.5
    low, high = 0.5 - r, 0.5 + r
    w = (0.5 * low * low, 0.75 - r * r, 0.5 * high * high)
    d = ((-1.0 - r) * w[0], -r * w[1], (1.0 - r) * w[2])
    return w, d


def place(where_at, first, values):
    k = where_at - first
    out = jnp.where(k == 2.0, values[2], 0.0)
    out = jnp.where(k == 1.0, values[1], out)
    return jnp.where(k == 0.0, values[0], out)


def halves(value):
    high = value.astype(BF16)
    return high, (value - high.astype(F32)).astype(BF16)


def prepare(cell, frac, planes, kept, mass, vel, stress, nby, nbz):
    wx, _ = spline(frac[0])
    wy, _ = spline(frac[1])
    wz, dz = spline(frac[2])
    at_x = (cell >> 4).astype(F32)
    at_y = ((cell >> 2) & 3).astype(F32)
    block = lax.broadcasted_iota(jnp.int32, cell.shape, 0)
    at_y = at_y + 4.0 * sum((block >= nbz * k).astype(F32) for k in range(1, nby))
    planes[YAT] = at_y
    planes[ZAT] = (cell & 3).astype(F32)
    for t in range(3):
        planes[WY + t] = wy[t]
        planes[WZ + t] = wz[t]
        planes[DZ + t] = dz[t]
    here = [at_x == float(k) for k in range(4)]
    for x in range(6):
        w = jnp.zeros_like(at_x)
        for k in range(max(0, x - 2), min(4, x + 1)):
            w = jnp.where(here[k], wx[x - k], w)
        planes[WX + x] = w
    position = (at_x + (frac[0] - 2.0), at_y + (frac[1] - 2.0 * nby))
    kept[XC] = position[0]
    kept[YC] = position[1]
    scaled = (4.0 * time_step) * stress
    planes[CHANNEL] = mass
    planes[CHANNEL + 1] = mass * vel[0] - scaled * position[0]
    planes[CHANNEL + 2] = mass * vel[1] - scaled * position[1]
    planes[CHANNEL + 3] = mass * vel[2]
    planes[CHANNEL + 4] = scaled


def z_rows(q):
    return 4 * q // 8 * 8, (4 * q + 5) // 8 * 8 + 8


def block_row(h, b, nbz):
    return b // GROUP * nbz + h * GROUP + b % GROUP


def deposit(planes, tiles, factors, sums, out, nby, nbz):
    sums[...] = jnp.zeros_like(sums)
    blocks = nby * GROUP

    def group(h, carry):
        columns, lines = [], []
        for b in range(blocks):
            row, q = block_row(h, b, nbz), b % GROUP
            get = lambda k: planes[k, pl.ds(row, 8, stride=0), :]
            at = lax.broadcasted_iota(jnp.int32, (8, 128), 0).astype(F32)
            wy = place(at, get(YAT) - 1.0, [get(WY + t) for t in range(3)])
            pieces = []
            for x in range(0, 6, 2):
                high, low = halves(jnp.concatenate([get(WX + x) * wy, get(WX + x + 1) * wy], axis=0))
                tiles[row, 8 * x : 8 * x + 16] = high
                tiles[row, 48 + 8 * x : 64 + 8 * x] = low
                pieces.append((high, low))
            lines.append(jnp.concatenate([p[0] for p in pieces] + [p[1] for p in pieces], axis=0))
            first, last = z_rows(q)
            steps = (last - first) // 8
            get = lambda k: jnp.concatenate([planes[k, pl.ds(row, 8, stride=0), :]] * steps, axis=0)
            at = lax.broadcasted_iota(jnp.int32, (last - first, 128), 0).astype(F32)
            start = get(ZAT) + float(4 * q - first)
            wz = place(at, start, [get(WZ + t) for t in range(3)])
            dz = place(at, start, [get(DZ + t) for t in range(3)])
            factors[row, 0, 0 : last - first] = wz
            factors[row, 1, 0 : last - first] = dz
            parts = [get(CHANNEL + c) * wz for c in range(CHANNELS)]
            parts[3] = parts[3] + get(CHANNEL + 4) * dz
            zeros = lambda n: [jnp.zeros((n, 128), F32)] if n else []
            high = [part.astype(BF16).astype(F32) for part in parts]
            low = [part - h for part, h in zip(parts, high)]
            stack = []
            for values in (high, low):
                for value in values:
                    stack += zeros(first) + [value] + zeros(WINDOW - last)
                stack += zeros(128 - CHANNELS * WINDOW)
            columns.append(jnp.concatenate(stack, axis=0).astype(BF16))
        a = jnp.concatenate(lines, axis=1)
        o = lax.dot_general(a, jnp.concatenate(columns, axis=1), (((1,), (1,)), ((), ())),
                            preferred_element_type=F32)
        o = o[0:48] + o[48:96]
        o = o[:, 0:128] + o[:, 128:256]
        z = lax.broadcasted_iota(jnp.int32, o.shape, 1) - (4 * GROUP * h - EDGE)
        inside = (z >= 0) & (z < WINDOW)
        for c in range(CHANNELS):
            moved = pltpu.roll(o, lax.rem(4 * GROUP * h + (128 - EDGE + 128 - WINDOW * c), 128), 1)
            sums[c] += jnp.where(inside, moved, 0.0)
        return carry

    lax.fori_loop(0, nbz // GROUP, group, 0, unroll=True)
    shape = out.shape[1:]
    x = lax.broadcasted_iota(jnp.int32, shape, 0).astype(F32) - 2.5
    y = lax.broadcasted_iota(jnp.int32, shape, 1).astype(F32) + (0.5 - 2.0 * nby)
    mass, mx, my, mz, stress = (sums[c].reshape(shape) for c in range(CHANNELS))
    out[0] = mass
    out[1] = mx + x * stress
    out[2] = my + y * stress
    out[3] = mz


def gather(vel, tiles, factors, turned, sampled, nby, nbz):
    blocks = nby * GROUP
    shape = vel[0].shape
    x = lax.broadcasted_iota(jnp.int32, shape, 0).astype(F32) - 2.5
    y = lax.broadcasted_iota(jnp.int32, shape, 1).astype(F32) + (0.5 - 2.0 * nby)
    for c, v in enumerate((vel[0], vel[1], vel[2], x * vel[0] + y * vel[1])):
        v = v.reshape(48, 128)
        high = v.astype(BF16).astype(F32)
        v = jnp.concatenate([high, v - high, jnp.zeros((32, 128), F32)], axis=0)
        turned[c, 0:8] = jnp.zeros((8, 128), F32)
        turned[c, 128:152] = jnp.zeros((24, 128), F32)
        turned[c, EDGE : EDGE + 128] = v.T
    pad = jnp.zeros((32, 128), F32).astype(BF16)

    def group(h, carry):
        at = pl.multiple_of(4 * GROUP * h, 8)
        v = jnp.concatenate([turned[c, pl.ds(at, WINDOW)] for c in range(4)], axis=0).astype(BF16)
        rows = [block_row(h, b, nbz) for b in range(blocks)]
        stack = []
        for part in (0, 48):
            piece = jnp.concatenate([tiles[row, part : part + 48] for row in rows], axis=1)
            stack += [piece, piece, jnp.concatenate([pad] * blocks, axis=1)]
        t = jnp.dot(jnp.concatenate([v, v], axis=1), jnp.concatenate(stack, axis=0), preferred_element_type=F32)
        for b, row in enumerate(rows):
            first, last = z_rows(b % GROUP)
            w, d = factors[row, 0, 0 : last - first], factors[row, 1, 0 : last - first]
            read = lambda c: t[WINDOW * c + first : WINDOW * c + last, 128 * b : 128 * b + 128]
            vz = read(2)
            for c, value in enumerate((w * read(0), w * read(1), w * vz, w * read(3) + d * vz)):
                sampled[c, pl.ds(row, 1), :] = jnp.sum(value, axis=0, keepdims=True)
        return carry

    lax.fori_loop(0, nbz // GROUP, group, 0, unroll=True)


def node_velocity(fields):
    mass = fields[0]
    inverse = 1.0 / jnp.maximum(mass, mass_floor)
    vel = [fields[k] * inverse for k in (1, 2, 3)]
    lifted = vel[2] - time_step * gravity
    floor = lax.broadcasted_iota(jnp.int32, lifted.shape, 2) == 0
    vel[2] = jnp.where(floor, jnp.maximum(lifted, 0.0), lifted)
    return mass, vel


def dragged(mass, vel, other_mass, other_vel, coef):
    slip = [b - a for a, b in zip(vel, other_vel)]
    rate = coef * jnp.sqrt(slip[0] * slip[0] + slip[1] * slip[1] + slip[2] * slip[2] + slip_floor)
    share = rate / (1.0 + rate) * (other_mass / (mass + other_mass + mass_floor))
    return [a + share * s for a, s in zip(vel, slip)]


class Side:
    def __init__(self):
        place_id = lax.axis_index("space")
        self.even = lax.rem(place_id, 2) == 0
        self.has_left = place_id > 0
        self.has_right = place_id < lax.axis_size("space") - 1

    def arrived(self, first, second, rows):
        first, second = first[rows], second[rows]
        from_left = jnp.where(self.even, second, first)
        from_right = jnp.where(self.even, first, second)
        return jnp.where(self.has_left, from_left, 0.0), jnp.where(self.has_right, from_right, 0.0)

    def layers(self, own, first, second):
        left, right = self.arrived(first, second, slice(0, 8))
        shape = (4, 2) + left.shape[1:]
        own = own[...]
        return jnp.concatenate(
            [own[:, 0:2] + left.reshape(shape), own[:, 2:4], own[:, 4:6] + right.reshape(shape)], axis=1
        )

    def send(self, own, first, second, coef=None):
        toward = jnp.where(self.even, 4, 0)
        for ref, start in ((first, toward), (second, 4 - toward)):
            for c in range(4):
                ref[2 * c : 2 * c + 2] = own[c, pl.ds(start, 2)]
        if coef is not None:
            first[8] = jnp.where(self.even, coef[3], coef[0])
            second[8] = jnp.where(self.even, coef[0], coef[3])

    def keep(self, vel):
        layer = lax.broadcasted_iota(jnp.int32, vel.shape, 0)
        keep = ((layer > 0) | self.has_left) & ((layer < vel.shape[0] - 1) | self.has_right)
        return jnp.where(keep, vel, 0.0)


def live_mask(count, shape):
    square = (shape[0], shape[0])
    same = lax.broadcasted_iota(jnp.int32, square, 0) == lax.broadcasted_iota(jnp.int32, square, 1)
    column = jnp.sum(jnp.where(same, count[...].astype(F32), 0.0), axis=1, keepdims=True)
    return lax.broadcasted_iota(jnp.int32, shape, 1).astype(F32) < column


def advance(sampled, kept, frac_ref, vel_ref, stress_ref):
    live = kept[LIVE] > 0.5
    vel = [sampled[k] for k in range(3)]
    rate = sampled[3] - kept[XC] * vel[0] - kept[YC] * vel[1]
    old = stress_ref[...]
    stress = jnp.where(live, old - (time_step * bulk_modulus * 4.0) * rate, old)
    frac = [jnp.where(live, frac_ref[k] + time_step * vel[k], frac_ref[k]) for k in range(3)]
    vel = [jnp.where(live, vel[k], vel_ref[k]) for k in range(3)]
    return frac, vel, stress


def store_state(state, new_frac, new_vel, new_stress):
    frac, vel, stress = state
    for k in range(3):
        new_frac[k] = frac[k]
        new_vel[k] = vel[k]
    new_stress[...] = stress


def first_kernel(sizes, *refs):
    sources, inputs, rest = refs[:7], refs[7:14], refs[14:]
    kept, tiles, factors, dep, first, second, planes, sums, sems = rest
    copies = [pltpu.make_async_copy(a, b, sems.at[k]) for k, (a, b) in enumerate(zip(sources, inputs))]
    for copy in copies:
        copy.start()
    for copy in copies:
        copy.wait()
    cell, count, frac, vel, mass, stress, coef = inputs
    live = live_mask(count, cell.shape)
    kept[LIVE] = jnp.where(live, 1.0, 0.0)
    m = jnp.where(live, mass[...], 0.0)
    s = jnp.where(live, stress[...], 0.0)
    prepare(cell[...], [frac[k] for k in range(3)], planes, kept, m, [vel[k] for k in range(3)], s, *sizes)
    deposit(planes, tiles, factors, sums, dep, *sizes)
    Side().send(dep, first, second, coef)


def total_kernel(dep, first, second, fields):
    fields[...] = Side().layers(dep, first, second)


def middle_kernel(sizes, cell, frac, vel, mass, stress, coef, kept, tiles, factors, fields, other, first, second,
                  new_frac, new_vel, new_stress, new_kept, new_tiles, new_factors, dep, new_first, new_second,
                  planes, sums, turned, sampled):
    side = Side()
    own_mass, own_vel = node_velocity(fields)
    other_mass, other_vel = node_velocity(other)
    low, high = side.arrived(first, second, slice(8, 9))
    coefs = jnp.concatenate([low, coef[...], high], axis=0)
    nodes = [side.keep(v) for v in dragged(own_mass, own_vel, other_mass, other_vel, coefs)]
    gather(nodes, tiles, factors, turned, sampled, *sizes)
    state = advance(sampled, kept, frac, vel, stress)
    store_state(state, new_frac, new_vel, new_stress)
    new_kept[LIVE] = kept[LIVE]
    live = kept[LIVE] > 0.5
    m = jnp.where(live, mass[...], 0.0)
    s = jnp.where(live, state[2], 0.0)
    prepare(cell[...], state[0], planes, new_kept, m, state[1], s, *sizes)
    deposit(planes, new_tiles, new_factors, sums, dep, *sizes)
    side.send(dep, new_first, new_second)


def last_kernel(sizes, frac, vel, stress, kept, tiles, factors, dep, first, second,
                new_frac, new_vel, new_stress, turned, sampled):
    side = Side()
    _, nodes = node_velocity(side.layers(dep, first, second))
    gather([side.keep(v) for v in nodes], tiles, factors, turned, sampled, *sizes)
    store_state(advance(sampled, kept, frac, vel, stress), new_frac, new_vel, new_stress)


def call(kernel, outs, scratch, *args, space=pltpu.VMEM, cost=None, limit=24 << 20):
    spec = pl.BlockSpec(memory_space=space)
    vmem = pl.BlockSpec(memory_space=pltpu.VMEM)
    return pl.pallas_call(
        kernel,
        out_shape=[jax.ShapeDtypeStruct(*(s if isinstance(s[0], tuple) else (s, F32))) for s in outs],
        in_specs=[spec] * len(args),
        out_specs=[vmem] * len(outs),
        scratch_shapes=scratch,
        cost_estimate=cost,
        compiler_params=pltpu.CompilerParams(vmem_limit_bytes=limit),
    )(*args)


def local(particle_cell, block_count, particle_frac, particle_vel, particle_mass, particle_stress, drag_coef):
    cell, count = particle_cell[0], block_count
    frac, vel = particle_frac[0], particle_vel[0]
    mass, stress = particle_mass[0], particle_stress[0]
    layers, ny, nz = drag_coef.shape
    sizes = nby, nbz = ny // 4, nz // 4
    blocks, slots = cell.shape
    places = lax.axis_size("space")

    def matching(start):
        pairs = [(i, i) for i in range(start)]
        for i in range(start, places - 1, 2):
            pairs += [(i, i + 1), (i + 1, i)]
        return pairs + [(i, i) for i in range(len(pairs), places)]

    swap = [(i, i ^ 1) for i in range(lax.axis_size("phase"))]
    particle = (blocks, slots)
    triple = (3,) + particle
    grid = (4, layers + 2, ny, nz)
    saved = [triple, ((blocks, 96, slots), BF16), (blocks, 2, 16, slots)]
    planes = pltpu.VMEM((PLANES,) + particle, F32)
    sums = pltpu.VMEM((CHANNELS, (layers + 2) * ny, nz), F32)
    turned = pltpu.VMEM((4, nz + 24, 128), F32)
    sampled = pltpu.VMEM((4,) + particle, F32)

    def exchange(first, second):
        second = lax.ppermute(second, "space", matching(1))
        first = lax.ppermute(first, "space", matching(0))
        return first, second

    inputs = (cell, count, frac, vel, mass, stress, drag_coef)
    sent = (9, ny, nz)
    *loaded, kept, tiles, factors, dep, first, second = call(
        functools.partial(first_kernel, sizes),
        [(a.shape, a.dtype) for a in inputs] + saved + [grid, sent, sent],
        [planes, sums, pltpu.SemaphoreType.DMA((7,))],
        *[pltpu.with_memory_space_constraint(a, pltpu.HBM) for a in inputs], space=pltpu.HBM)
    first, second = exchange(first, second)
    fields, = call(total_kernel, [grid], [], dep, first, second)
    other = lax.ppermute(fields, "phase", swap)
    sent = (8, ny, nz)
    frac, vel, stress, kept, tiles, factors, dep, first, second = call(
        functools.partial(middle_kernel, sizes),
        [triple, triple, particle] + saved + [grid, sent, sent],
        [planes, sums, turned, sampled],
        loaded[0], *loaded[2:], kept, tiles, factors, fields, other, first, second)
    first, second = exchange(first, second)
    frac, vel, stress = call(
        functools.partial(last_kernel, sizes), [triple, triple, particle], [turned, sampled],
        frac, vel, stress, kept, tiles, factors, dep, first, second)
    return frac[None], vel[None], stress[None]


def solution(mesh):
    in_specs = (
        P("phase", "space", None),
        P("phase", "space"),
        P("phase", None, "space", None),
        P("phase", None, "space", None),
        P("phase", "space", None),
        P("phase", "space", None),
        P("space", None, None),
    )
    out_specs = (
        P("phase", None, "space", None),
        P("phase", None, "space", None),
        P("phase", "space", None),
    )
    return jax.shard_map(local, mesh=mesh, in_specs=in_specs, out_specs=out_specs, check_vma=False)
```
